32 devices in a mesh: gy: 16 (over z, x, core), gx: 2 (over y).
Axes of the slice: x: 2, y: 2, z: 4, core: 2. Of those that a mesh axis runs over, the one named last changes fastest.
Arguments:
- level_set: float32 [1024, 1024], P('gy', 'gx'), may hold values from -6 to 6
- velocity: float32 [2, 1024, 1024], P(None, 'gy', 'gx'), may hold values from -2 to 2
- particles: float32 [2048, 3, 128], P(('gy', 'gx')), may hold values from -0.5 to 0.5
- escaped: int32 [2048, 128], P(('gy', 'gx')), may hold values 0 or 1
- home_cell: int32 [2048], P(('gy', 'gx')), may hold values from 0 to 32767
- land_cell: int32 [2048], P(('gy', 'gx')), may hold values from 0 to 32767
- dest_rank: int32 [2048], P(('gy', 'gx')), may hold values from 0 to 15, as said below
- block_count: int32 [32], P(('gy', 'gx')), may hold values from 48 to 64, as said below
Outputs:
- new_level: float32 [1024, 1024], P('gy', 'gx')
- moved_blocks: float32 [2048, 4, 128], P(('gy', 'gx'))
The draws below stay inside these ranges and needn't reach their ends.
Inputs may be any that keep to these rules, and one draw needn't show every extreme that they name: `block_count`: live blocks are the first ones of a device; in every draw some device holds 64 live blocks. `dest_rank`: among one device's live blocks at most 4 go to one band; in every draw one band receives exactly 4 live blocks from every device.
All inputs are finite; a program needn't handle non-finite values. No bound on the sum of `escaped` on one device may be relied on, other than what follows from the above.
Results may differ from the reference program's by a relative error of at most 0.0003.
Values sent between devices are 32-bit elements; how exact they have to be, the bound alone decides.
A program may use at most 64 MiB of HBM per device.

```python
import math
import jax
import jax.numpy as jnp
from jax import lax

CY = 64
CX = 512
NB_DEV = 64
PPB = 128
CAP = 4
NY = 1024
NX = 1024
BLOCKS = 2048
RECV = 2048
N_GY = 16
N_GX = 2
DEVICES = 32


def migration_plan(key):
    slot_count = N_GY * CAP
    hot_band = jax.random.randint(jax.random.fold_in(key, 7), (), 0, N_GY)
    is_hot = (jnp.arange(slot_count, dtype=jnp.int32) // CAP == hot_band).astype(jnp.int32)

    def one_device(device_index):
        subkeys = jax.random.split(jax.random.fold_in(key, 1000 + device_index), 4)
        scores = (jax.random.randint(subkeys[0], (slot_count,), 0, 2 ** 20) + is_hot * 2 ** 22) * slot_count
        scores = scores + jnp.arange(slot_count, dtype=jnp.int32)
        chosen = jnp.argsort(-scores)[:NB_DEV] // CAP
        halfway = NB_DEV // 2
        front_part = jax.random.permutation(subkeys[1], chosen[:halfway])
        back_part = jax.random.permutation(subkeys[2], chosen[halfway:])
        live_total = jax.random.randint(subkeys[3], (), NB_DEV - NB_DEV // 4, NB_DEV + 1)
        return (jnp.concatenate([front_part, back_part]), live_total)
    destinations, tallies = jax.vmap(one_device)(jnp.arange(DEVICES, dtype=jnp.int32))
    filled_device = jax.random.randint(jax.random.fold_in(key, 9), (), 0, DEVICES)
    tallies = jnp.where(jnp.arange(DEVICES, dtype=jnp.int32) == filled_device, NB_DEV, tallies)
    return (destinations.reshape(-1).astype(jnp.int32), tallies.astype(jnp.int32))


def cell_draw(key):
    subkeys = jax.random.split(key, 4)
    row_pick = jax.random.randint(subkeys[0], (BLOCKS,), 0, CY)
    column_pick = jax.random.randint(subkeys[1], (BLOCKS,), 0, CX)
    row_pick = jnp.where(jax.random.randint(subkeys[2], (BLOCKS,), 0, 4) == 0, CY - 1, row_pick)
    column_pick = jnp.where(jax.random.randint(subkeys[3], (BLOCKS,), 0, 4) == 0, CX - 1, column_pick)
    return (row_pick * CX + column_pick).astype(jnp.int32)


def draw_dest_rank(key, part):
    return migration_plan(key)[0]


def draw_block_count(key, part):
    return migration_plan(key)[1]


def draw_home_cell(key, part):
    return cell_draw(jax.random.fold_in(key, 21))


def draw_land_cell(key, part):
    return cell_draw(jax.random.fold_in(key, 22))


def draw_level_set(key, part):
    subkeys = jax.random.split(jax.random.fold_in(key, 31), 2)
    row_global = jnp.arange(NY, dtype=jnp.int32)[:, None]
    column_global = jnp.arange(NX, dtype=jnp.int32)[None, :]
    row_local = row_global % CY
    column_local = column_global % CX
    near_edge = (row_local < 9) | (row_local >= CY - 9) | (column_local < 9) | (column_local >= CX - 9)
    parity = ((row_global + column_global) % 2 * 2 - 1).astype(jnp.float32)
    magnitude = jnp.clip(1.0 + 2.0 * jnp.abs(jax.random.normal(subkeys[0], (NY, NX), jnp.float32)), 1.0, 6.0)
    flipped = jax.random.uniform(subkeys[1], (NY, NX), jnp.float32) < 0.25
    signed = jnp.where(flipped, -1.0, 1.0) * parity * magnitude
    return jnp.where(near_edge, signed, 0.05 * signed).astype(jnp.float32)


def draw_velocity(key, part):
    subkeys = jax.random.split(jax.random.fold_in(key, 41), 2)
    magnitude = jax.random.uniform(subkeys[0], (2, NY, NX), jnp.float32, 1.0, 2.0)
    positive = jax.random.uniform(subkeys[1], (2, NY, NX), jnp.float32) < 0.5
    return jnp.where(positive, magnitude, -magnitude).astype(jnp.float32)


def set_ends(values, stream_key, low, largest):
    dims = values.shape
    place = [jax.random.randint(jax.random.fold_in(stream_key, axis), (), 0, dims[axis]) for axis in range(len(dims))]
    values = values.at[tuple(place)].set(low)
    longest = dims.index(max(dims))
    place[longest] = (place[longest] + 1) % dims[longest]
    return values.at[tuple(place)].set(largest)


def steps_of(rng, extent, cuts, low, high):
    level, own = 1.0, jax.random.fold_in(rng, 6)
    for dim, blocks in cuts:
        steps = jnp.exp(jax.random.uniform(jax.random.fold_in(own, dim), (blocks,), jnp.float32, low / len(cuts), high / len(cuts)))
        level = level * jnp.repeat(steps, extent[dim] // blocks).reshape([-1 if axis == dim else 1 for axis in range(len(extent))])
    return level


def setup_inputs(seed: int = 0) -> dict:
    key_of = jax.random.split(jax.random.key(seed), 9)
    level_set = draw_level_set(jax.random.fold_in(key_of[8], 71), 0)
    velocity = draw_velocity(jax.random.fold_in(key_of[8], 71), 0)
    particles = jnp.clip(jax.random.uniform(key_of[2], (BLOCKS, 3, PPB), jnp.float32, -0.5, 0.5) * steps_of(key_of[2], (BLOCKS, 3, PPB), ((0, 32),), -0.4, 0.0), -0.5, 0.5)
    escaped = set_ends((jax.random.randint(key_of[3], (BLOCKS, PPB), 0, 2) < 1).astype(jnp.int32), jax.random.fold_in(key_of[3], 1), 0, 1)
    home_cell = draw_home_cell(jax.random.fold_in(key_of[8], 71), 0)
    land_cell = draw_land_cell(jax.random.fold_in(key_of[8], 71), 0)
    dest_rank = draw_dest_rank(jax.random.fold_in(key_of[8], 71), 0)
    block_count = draw_block_count(jax.random.fold_in(key_of[8], 71), 0)
    return dict(level_set=level_set, velocity=velocity, particles=particles, escaped=escaped, home_cell=home_cell, land_cell=land_cell, dest_rank=dest_rank, block_count=block_count)


time_step = 0.3
epsilon_weno = 1e-6


def blended(a, b, c, d, e):
    smooth_one = 13.0 / 12.0 * (a - 2.0 * b + c) ** 2 + 0.25 * (a - 4.0 * b + 3.0 * c) ** 2
    smooth_two = 13.0 / 12.0 * (b - 2.0 * c + d) ** 2 + 0.25 * (b - d) ** 2
    smooth_three = 13.0 / 12.0 * (c - 2.0 * d + e) ** 2 + 0.25 * (3.0 * c - 4.0 * d + e) ** 2
    weight_one = 0.1 / (smooth_one + epsilon_weno) ** 2
    weight_two = 0.6 / (smooth_two + epsilon_weno) ** 2
    weight_three = 0.3 / (smooth_three + epsilon_weno) ** 2
    weight_sum = weight_one + weight_two + weight_three
    candidate = (weight_one * (a / 3.0 - 7.0 * b / 6.0 + 11.0 * c / 6.0)
                 + weight_two * (-b / 6.0 + 5.0 * c / 6.0 + d / 3.0)
                 + weight_three * (c / 3.0 + 5.0 * d / 6.0 - e / 6.0))
    return candidate / weight_sum


def upwinded(shifted, advecting):
    differences = [shifted(k + 1) - shifted(k) for k in range(-3, 3)]
    left_sided = blended(differences[0], differences[1], differences[2], differences[3], differences[4])
    right_sided = blended(differences[5], differences[4], differences[3], differences[2], differences[1])
    return advecting * jnp.where(advecting > 0, left_sided, right_sided)


def tendency(padded, along_x, along_y):
    height = along_x.shape[0]
    across = along_x.shape[1]

    def columns(k):
        return padded[3:3 + height, 3 + k:3 + k + across]

    def rows_at(k):
        return padded[3 + k:3 + k + height, 3:3 + across]

    return -(upwinded(columns, along_x) + upwinded(rows_at, along_y))


def full_tendency(surface, velocity):
    padded = jnp.pad(surface, 3, mode="wrap")
    band_rows = math.gcd(NY, 256)

    def one_band(start):
        window = lax.dynamic_slice_in_dim(padded, start, band_rows + 6, 0)
        along_x = lax.dynamic_slice_in_dim(velocity[0], start, band_rows, 0)
        along_y = lax.dynamic_slice_in_dim(velocity[1], start, band_rows, 0)
        return tendency(window, along_x, along_y)

    starts = jnp.arange(NY // band_rows, dtype=jnp.int32) * band_rows
    return lax.map(one_band, starts).reshape(NY, NX)


def advect(offset_x, offset_y, corners):
    fraction_y = offset_y + 0.5
    fraction_x = offset_x + 0.5

    def mixture(component):
        c = corners[:, component]
        return ((1.0 - fraction_y) * (1.0 - fraction_x) * c[:, 0:1] + fraction_y * (1.0 - fraction_x) * c[:, 1:2]
                + (1.0 - fraction_y) * fraction_x * c[:, 2:3] + fraction_y * fraction_x * c[:, 3:4])

    return offset_x + time_step * mixture(0), offset_y + time_step * mixture(1)


def reference(level_set, velocity, particles, escaped, home_cell, land_cell, dest_rank, block_count):
    section_one = level_set + time_step * full_tendency(level_set, velocity)
    section_two = 0.75 * level_set + 0.25 * (section_one + time_step * full_tendency(section_one, velocity))
    section_three = level_set / 3.0 + 2.0 / 3.0 * (section_two + time_step * full_tendency(section_two, velocity))

    blocks = jnp.arange(BLOCKS, dtype=jnp.int32)
    device = blocks // NB_DEV
    band_index = device // N_GX
    strip_index = device % N_GX
    local_index = blocks % NB_DEV
    is_live = local_index < block_count[device]
    home_row = band_index * CY + home_cell // CX
    home_column = strip_index * CX + home_cell % CX
    next_row = (home_row + 1) % NY
    next_column = (home_column + 1) % NX
    corners = jnp.stack([velocity[:, home_row, home_column], velocity[:, next_row, home_column],
                         velocity[:, home_row, next_column], velocity[:, next_row, next_column]], axis=-1)
    corners = jnp.transpose(corners, (1, 0, 2))
    new_x, new_y = advect(particles[:, 0, :], particles[:, 1, :], corners)
    radius = particles[:, 2, :]
    weight = escaped.astype(jnp.float32) * radius
    moved_rows = jnp.stack([new_x, new_y, radius, weight], axis=1)

    grouped = dest_rank.reshape(DEVICES, NB_DEV)
    live_grid = is_live.reshape(DEVICES, NB_DEV)
    position = jnp.arange(NB_DEV, dtype=jnp.int32)
    earlier_same = ((grouped[:, None, :] == grouped[:, :, None]) & live_grid[:, None, :]
                    & (position[None, :] < position[:, None])[None])
    slot_rank = jnp.sum(earlier_same.astype(jnp.int32), axis=2).reshape(-1)
    target = (dest_rank * N_GX + strip_index) * (N_GY * CAP) + band_index * CAP + slot_rank
    target = jnp.where(is_live, target, RECV)
    moved_blocks = jnp.zeros((RECV, 4, PPB), jnp.float32).at[target].set(moved_rows, mode="drop")

    land_row = dest_rank * CY + land_cell // CX
    land_next = (land_row + 1) % NY
    land_column = strip_index * CX + land_cell % CX
    land_right = (land_column + 1) % NX
    fraction_y = new_y + 0.5
    fraction_x = new_x + 0.5
    carried = weight * is_live.astype(jnp.float32)[:, None]
    low_low = jnp.sum(carried * (1.0 - fraction_y) * (1.0 - fraction_x), axis=1)
    high_low = jnp.sum(carried * fraction_y * (1.0 - fraction_x), axis=1)
    low_high = jnp.sum(carried * (1.0 - fraction_y) * fraction_x, axis=1)
    high_high = jnp.sum(carried * fraction_y * fraction_x, axis=1)
    deposit = jnp.zeros((NY, NX), jnp.float32)
    deposit = deposit.at[land_row, land_column].add(low_low)
    deposit = deposit.at[land_next, land_column].add(high_low)
    deposit = deposit.at[land_row, land_right].add(low_high)
    deposit = deposit.at[land_next, land_right].add(high_high)
    return section_three + deposit, moved_blocks
```

```python
import functools

import jax
import jax.numpy as jnp
from jax import lax
from jax.experimental import pallas as pl
from jax.experimental.pallas import tpu as pltpu
from jax.sharding import PartitionSpec as P

CAP = 4
FIELDS = 4
STEP = 0.3
EPS4 = 4e-06
LANES = 128
DEEP = 16
THIN = 8
MESH = pl.DeviceIdType.MESH
EXACT = lax.Precision.HIGHEST


def one_sided(speed, lower, upper, s_m2, s_m1, s_0, s_p1, s_p2):
    ahead = speed > 0
    c = jnp.where(ahead, lower, upper)
    p = jnp.where(ahead, s_m2, s_p2)
    q = jnp.where(ahead, s_m1, s_p1)
    r = s_0
    w = jnp.where(ahead, s_p1, s_m1)
    k = 13.0 / 3.0
    a1, b1 = p - q, p - 3.0 * q
    a2, b2 = q - r, q + r
    a3, b3 = r - w, 3.0 * r - w
    t1 = k * (a1 * a1) + (b1 * b1 + EPS4)
    t2 = k * (a2 * a2) + (b2 * b2 + EPS4)
    t3 = k * (a3 * a3) + (b3 * b3 + EPS4)
    m1, m2, m3 = t2 * t3, t1 * t3, t1 * t2
    w1 = m1 * m1
    w2 = 6.0 * (m2 * m2)
    w3 = 3.0 * (m3 * m3)
    top = w1 * (2.0 * p - 5.0 * q) - w2 * (q + 2.0 * r) + w3 * (w - 4.0 * r)
    bottom = w1 + w2 + w3
    return speed * c - (jnp.abs(speed) * (1.0 / 6.0)) * (top / bottom)


def step_term(field, row, u, v):
    window = field[pl.ds(pl.multiple_of(row - 8, 8), 24), :]
    taps = [pltpu.roll(window, (24 - k) % 24, 0)[8:16] for k in range(-3, 4)]
    here = taps[3]
    width = here.shape[1]
    d = [taps[k + 1] - taps[k] for k in range(6)]
    s = [d[k + 1] - d[k] for k in range(5)]
    along_y = one_sided(v, d[2], d[3], *s)
    upper = pltpu.roll(here, width - 1, 1) - here
    lower = here - pltpu.roll(here, 1, 1)
    mid = upper - lower
    along_x = one_sided(
        u,
        lower,
        upper,
        pltpu.roll(mid, 2, 1),
        pltpu.roll(mid, 1, 1),
        mid,
        pltpu.roll(mid, width - 1, 1),
        pltpu.roll(mid, width - 2, 1),
    )
    return here, -(along_x + along_y)


def kernel(
    nb,
    nx,
    level_hbm,
    flow_hbm,
    parts_hbm,
    escaped_hbm,
    home_ref,
    land_ref,
    dest_ref,
    count_ref,
    out_ref,
    moved_hbm,
    f0,
    flow,
    f1,
    f2,
    side,
    from_left,
    from_right,
    parts,
    escaped,
    packed,
    records,
    rec_same,
    rec_left,
    load_sem,
    halo_send,
    halo_recv,
    pay_send,
    pay_recv,
    rec_send,
    rec_recv,
    left_send,
    left_recv,
    own_sem,
):
    g = lax.axis_index("gy")
    s = lax.axis_index("gx")
    height, across = level_hbm.shape
    width = across + LANES
    total = parts_hbm.shape[0]
    up = lax.rem(g + nb - 1, nb)
    down = lax.rem(g + 1, nb)
    left = lax.rem(s + nx - 1, nx)
    right = lax.rem(s + 1, nx)

    barrier = pltpu.get_barrier_semaphore()
    offsets = sorted({0, 1 % nx, (nx - 1) % nx})
    for off in offsets:
        strip = lax.rem(s + off, nx)

        def greet(k, carry, strip=strip):
            pl.semaphore_signal(
                barrier, inc=1, device_id=(lax.rem(g + k, nb), strip), device_id_type=MESH
            )
            return carry

        lax.fori_loop(1 if off == 0 else 0, nb, greet, 0)

    loads = [
        pltpu.make_async_copy(
            level_hbm, f0.at[pl.ds(DEEP, height), pl.ds(0, across)], load_sem.at[0]
        ),
        pltpu.make_async_copy(
            flow_hbm, flow.at[:, pl.ds(THIN, height), pl.ds(0, across)], load_sem.at[1]
        ),
        pltpu.make_async_copy(parts_hbm, parts, load_sem.at[2]),
        pltpu.make_async_copy(escaped_hbm, escaped, load_sem.at[3]),
    ]
    for copy in loads:
        copy.start()

    home = home_ref[...].reshape(1, total)
    land = land_ref[...].reshape(1, total)
    dest = dest_ref[...].reshape(1, total)
    lane = lax.broadcasted_iota(jnp.int32, (total, total), 1)
    sub = lax.broadcasted_iota(jnp.int32, (total, total), 0)

    def upright(row):
        return jnp.sum(jnp.where(lane == sub, row, 0), axis=1, keepdims=True)

    dest_col = upright(dest)
    home_col = upright(home)
    land_col = upright(land)
    live = count_ref[0]
    earlier = (dest == dest_col) & (sub < lane) & (sub < live)
    rank = jnp.sum(earlier.astype(jnp.int32), axis=0, keepdims=True)
    is_live = lax.broadcasted_iota(jnp.int32, (1, total), 1) < live
    slot = jnp.where(is_live, dest * (CAP * FIELDS) + rank * FIELDS, -64)
    own_row = jnp.where(is_live, dest * (2 * CAP) + rank, -64)
    next_band = jnp.where(dest == nb - 1, 0, dest + 1)
    past_row = jnp.where(is_live, next_band * (2 * CAP) + CAP + rank, -64)

    loads[0].wait()
    loads[1].wait()

    spot = lax.broadcasted_iota(jnp.int32, (height, LANES), 1)
    low = [
        f0[pl.ds(DEEP, height), 0:LANES],
        pltpu.roll(flow[0, pl.ds(THIN, height), 0:LANES], 16, 1),
        pltpu.roll(flow[1, pl.ds(THIN, height), 0:LANES], 32, 1),
    ]
    tail = pl.ds(across - LANES, LANES)
    high = [
        f0[pl.ds(DEEP, height), tail],
        pltpu.roll(flow[0, pl.ds(THIN, height), tail], LANES - 16, 1),
        pltpu.roll(flow[1, pl.ds(THIN, height), tail], LANES - 32, 1),
    ]
    low_edge = jnp.where(spot < 16, low[0], jnp.where(spot < 32, low[1], low[2]))
    high_edge = jnp.where(spot >= 112, high[0], jnp.where(spot >= 96, high[1], high[2]))
    side[...] = jnp.where(spot < 64, low_edge, high_edge)

    pl.semaphore_wait(barrier, nb * len(offsets) - 1)

    halo = []

    def send(src, dst, band, strip):
        i = len(halo)
        copy = pltpu.make_async_remote_copy(
            src_ref=src,
            dst_ref=dst,
            send_sem=halo_send.at[i],
            recv_sem=halo_recv.at[i],
            device_id=(band, strip),
            device_id_type=MESH,
        )
        copy.start()
        halo.append(copy)

    wide = pl.ds(0, across)
    for box, strip in ((from_right, left), (from_left, right))[: 2 if nx > 2 else 1]:
        send(side, box.at[pl.ds(DEEP, height)], g, strip)
        send(side.at[pl.ds(0, DEEP)], box.at[pl.ds(DEEP + height, DEEP)], up, strip)
        send(side.at[pl.ds(height - DEEP, DEEP)], box.at[pl.ds(0, DEEP)], down, strip)
    send(
        flow_hbm.at[:, pl.ds(0, THIN)], flow.at[:, pl.ds(THIN + height, THIN), wide], up, s
    )
    send(
        flow_hbm.at[:, pl.ds(height - THIN, THIN)], flow.at[:, pl.ds(0, THIN), wide], down, s
    )
    send(level_hbm.at[pl.ds(0, DEEP)], f0.at[pl.ds(DEEP + height, DEEP), wide], up, s)
    send(level_hbm.at[pl.ds(height - DEEP, DEEP)], f0.at[pl.ds(0, DEEP), wide], down, s)

    loads[2].wait()
    loads[3].wait()
    radius = parts[:, 2, :]
    weight = escaped[...].astype(jnp.float32) * radius

    home_row = home_col // across
    home_at = home_col - home_row * across
    pick_lane = lax.broadcasted_iota(jnp.int32, (total, THIN + height), 1)
    pick_this = (pick_lane == home_row).astype(jnp.float32)
    pick_next = (pick_lane == home_row + 1).astype(jnp.float32)

    for copy in halo:
        copy.wait()

    spot = lax.broadcasted_iota(jnp.int32, (height + 2 * DEEP, LANES), 1)
    after = from_right[...]
    before = from_left[...] if nx > 2 else after
    end = pl.ds(across, LANES)
    f0[:, end] = jnp.where(spot < 64, after, before)
    inner = slice(DEEP - THIN, DEEP + height + THIN)
    spot, after, before = spot[inner], after[inner], before[inner]
    flow[0, :, end] = jnp.where(
        spot < 64, pltpu.roll(after, LANES - 16, 1), pltpu.roll(before, 16, 1)
    )
    flow[1, :, end] = jnp.where(
        spot < 64, pltpu.roll(after, LANES - 32, 1), pltpu.roll(before, 32, 1)
    )

    column = lax.broadcasted_iota(jnp.int32, (total, width), 1)
    this_column = column == home_at
    next_column = column == home_at + 1

    fraction_y = parts[:, 1, :] + 0.5
    fraction_x = parts[:, 0, :] + 0.5

    def mixture(component):
        cells = flow[component, pl.ds(THIN, height + THIN), :]
        this_row = jnp.dot(
            pick_this, cells, precision=EXACT, preferred_element_type=jnp.float32
        )
        next_row = jnp.dot(
            pick_next, cells, precision=EXACT, preferred_element_type=jnp.float32
        )

        def at(rows, mask):
            return jnp.sum(jnp.where(mask, rows, 0.0), axis=1, keepdims=True)

        return (
            (1.0 - fraction_y) * (1.0 - fraction_x) * at(this_row, this_column)
            + fraction_y * (1.0 - fraction_x) * at(next_row, this_column)
            + (1.0 - fraction_y) * fraction_x * at(this_row, next_column)
            + fraction_y * fraction_x * at(next_row, next_column)
        )

    new_x = parts[:, 0, :] + STEP * mixture(0)
    new_y = parts[:, 1, :] + STEP * mixture(1)

    slot_row = lax.broadcasted_iota(jnp.int32, (nb * CAP * FIELDS, total), 0)
    payload = None
    for k, rows in enumerate((new_x, new_y, radius, weight)):
        term = jnp.dot(
            (slot_row == slot + k).astype(jnp.float32),
            rows,
            precision=EXACT,
            preferred_element_type=jnp.float32,
        )
        payload = term if payload is None else payload + term
    packed[...] = payload

    gy = new_y + 0.5
    gx = new_x + 0.5

    def over(rows):
        return jnp.sum(rows, axis=1, keepdims=True)

    land_row = land_col // across
    columns = (
        land_row.astype(jnp.float32),
        (land_col - land_row * across).astype(jnp.float32),
        over(weight * (1.0 - gy) * (1.0 - gx)),
        over(weight * gy * (1.0 - gx)),
        over(weight * (1.0 - gy) * gx),
        over(weight * gy * gx),
    )
    spot = lax.broadcasted_iota(jnp.int32, (total, LANES), 1)
    table = jnp.zeros((total, LANES), jnp.float32)
    for k, one in enumerate(columns):
        table = jnp.where(spot == k, one, table)
    rec_row = lax.broadcasted_iota(jnp.int32, (nb * 2 * CAP, total), 0)
    records[...] = jnp.dot(
        ((rec_row == own_row) | (rec_row == past_row)).astype(jnp.float32),
        table,
        precision=EXACT,
        preferred_element_type=jnp.float32,
    )

    per = CAP * FIELDS
    two = 2 * CAP
    mine = pl.ds(pl.multiple_of(g * per, per), per)
    mine_rec = pl.ds(pl.multiple_of(g * two, two), two)

    def pay_copy(k):
        peer = lax.rem(g + k, nb)
        return pltpu.make_async_remote_copy(
            src_ref=packed.at[pl.ds(pl.multiple_of(peer * per, per), per)],
            dst_ref=moved_hbm.at[mine],
            send_sem=pay_send.at[k],
            recv_sem=pay_recv.at[k],
            device_id=(peer, s),
            device_id_type=MESH,
        )

    def rec_copy(k):
        peer = lax.rem(g + k, nb)
        return pltpu.make_async_remote_copy(
            src_ref=records.at[pl.ds(pl.multiple_of(peer * two, two), two)],
            dst_ref=rec_same.at[mine_rec],
            send_sem=rec_send.at[k],
            recv_sem=rec_recv.at[k],
            device_id=(peer, s),
            device_id_type=MESH,
        )

    def left_copy(k):
        peer = lax.rem(g + k, nb)
        return pltpu.make_async_remote_copy(
            src_ref=records.at[pl.ds(pl.multiple_of(peer * two, two), two)],
            dst_ref=rec_left.at[mine_rec],
            send_sem=left_send.at[k],
            recv_sem=left_recv.at[k],
            device_id=(peer, right),
            device_id_type=MESH,
        )

    def start_far(k, carry):
        rec_copy(k).start()
        left_copy(k).start()
        pay_copy(k).start()
        return carry

    left_copy(0).start()
    lax.fori_loop(1, nb, start_far, 0)
    own = [
        pltpu.make_async_copy(packed.at[mine], moved_hbm.at[mine], own_sem.at[0]),
        pltpu.make_async_copy(records.at[mine_rec], rec_same.at[mine_rec], own_sem.at[1]),
    ]
    for copy in own:
        copy.start()

    def first(i, carry):
        row = pl.multiple_of(i * 8, 8)
        here, term = step_term(
            f0, row + DEEP - THIN, flow[0, pl.ds(row, 8), :], flow[1, pl.ds(row, 8), :]
        )
        f1[pl.ds(row + DEEP - THIN, 8), :] = here + STEP * term
        return carry

    lax.fori_loop(0, (height + 2 * THIN) // 8, first, 0)

    def second(i, carry):
        row = pl.multiple_of(i * 8, 8)
        here, term = step_term(
            f1, row + DEEP - THIN, flow[0, pl.ds(row, 8), :], flow[1, pl.ds(row, 8), :]
        )
        at = pl.ds(row + DEEP - THIN, 8)
        f2[at, :] = 0.75 * f0[at, :] + 0.25 * (here + STEP * term)
        return carry

    lax.fori_loop(0, (height + 2 * THIN) // 8, second, 0)

    def third(i, carry):
        row = pl.multiple_of(i * 8, 8)
        at = pl.ds(row + THIN, 8)
        here, term = step_term(f2, row + DEEP, flow[0, at, :], flow[1, at, :])
        value = f0[pl.ds(row + DEEP, 8), :] / 3.0 + 2.0 / 3.0 * (here + STEP * term)
        out_ref[pl.ds(row, 8), :] = value[:, :across]
        return carry

    lax.fori_loop(0, height // 8, third, 0)

    for copy in own:
        copy.wait()
    left_copy(0).wait()

    def finish_far(k, carry):
        rec_copy(k).wait()
        left_copy(k).wait()
        return carry

    lax.fori_loop(1, nb, finish_far, 0)

    count = nb * two
    row_lane = lax.broadcasted_iota(jnp.int32, (count, LANES), 1)
    which = lax.broadcasted_iota(jnp.int32, (count, 1), 0)
    shift = jnp.where(lax.rem(which, two) >= CAP, float(height), 0.0)
    row_lane = row_lane.astype(jnp.float32)
    lane_out = lax.broadcasted_iota(jnp.int32, (count, across), 1).astype(jnp.float32)

    def laid(hot, rows):
        return lax.dot_general(
            hot.astype(jnp.float32),
            rows,
            (((0,), (0,)), ((), ())),
            precision=EXACT,
            preferred_element_type=jnp.float32,
        )[:height]

    box = rec_same[...]
    row_of = box[:, 0:1] - shift
    col_of = box[:, 1:2]
    at_col = lane_out == col_of
    at_next = lane_out == col_of + 1.0
    same_low = jnp.where(at_col, box[:, 2:3], jnp.where(at_next, box[:, 4:5], 0.0))
    same_high = jnp.where(at_col, box[:, 3:4], jnp.where(at_next, box[:, 5:6], 0.0))
    out_ref[...] += laid(row_lane == row_of, same_low) + laid(
        row_lane == row_of + 1.0, same_high
    )
    box = rec_left[...]
    row_of = box[:, 0:1] - shift
    spill = (box[:, 1:2] == float(across - 1)) & (row_lane == 0.0)
    left_low = jnp.where(spill, box[:, 4:5], 0.0)
    left_high = jnp.where(spill, box[:, 5:6], 0.0)
    out_ref[:, 0:LANES] += laid(row_lane == row_of, left_low) + laid(
        row_lane == row_of + 1.0, left_high
    )

    def finish_pay(k, carry):
        pay_copy(k).wait()
        return carry

    lax.fori_loop(1, nb, finish_pay, 0)


def shards(nb, nx, level_set, velocity, particles, escaped, home, land, dest, count):
    height, across = level_set.shape
    total, _, per_block = particles.shape
    width = across + LANES
    rows = nb * CAP * FIELDS
    recs = nb * 2 * CAP
    halos = 10 if nx > 2 else 7
    anywhere = pl.BlockSpec(memory_space=pl.ANY)
    vmem = pl.BlockSpec(memory_space=pltpu.VMEM)
    smem = pl.BlockSpec(memory_space=pltpu.SMEM)
    f32 = jnp.float32
    dma = pltpu.SemaphoreType.DMA
    level, moved = pl.pallas_call(
        functools.partial(kernel, nb, nx),
        out_shape=(
            jax.ShapeDtypeStruct((height, across), f32),
            jax.ShapeDtypeStruct((rows, per_block), f32),
        ),
        in_specs=[anywhere] * 4 + [vmem] * 3 + [smem],
        out_specs=(vmem, anywhere),
        scratch_shapes=[
            pltpu.VMEM((height + 2 * DEEP, width), f32),
            pltpu.VMEM((2, height + 2 * THIN, width), f32),
            pltpu.VMEM((height + 2 * DEEP, width), f32),
            pltpu.VMEM((height + 2 * DEEP, width), f32),
            pltpu.VMEM((height, LANES), f32),
            pltpu.VMEM((height + 2 * DEEP, LANES), f32),
            pltpu.VMEM((height + 2 * DEEP, LANES), f32),
            pltpu.VMEM(particles.shape, f32),
            pltpu.VMEM(escaped.shape, jnp.int32),
            pltpu.VMEM((rows, per_block), f32),
            pltpu.VMEM((recs, LANES), f32),
            pltpu.VMEM((recs, LANES), f32),
            pltpu.VMEM((recs, LANES), f32),
            dma((4,)),
            dma((halos,)),
            dma((halos,)),
            dma((nb,)),
            dma((nb,)),
            dma((nb,)),
            dma((nb,)),
            dma((nb,)),
            dma((nb,)),
            dma((2,)),
        ],
        compiler_params=pltpu.CompilerParams(collective_id=0, has_side_effects=True),
    )(level_set, velocity, particles, escaped, home, land, dest, count)
    return level, moved.reshape(nb * CAP, FIELDS, per_block)


def solution(mesh):
    in_specs = (
        P("gy", "gx"),
        P(None, "gy", "gx"),
        P(("gy", "gx"), None, None),
        P(("gy", "gx"), None),
        P(("gy", "gx")),
        P(("gy", "gx")),
        P(("gy", "gx")),
        P(("gy", "gx")),
    )
    out_specs = (P("gy", "gx"), P(("gy", "gx"), None, None))
    body = functools.partial(shards, mesh.shape["gy"], mesh.shape["gx"])
    return jax.shard_map(body, mesh=mesh, in_specs=in_specs, out_specs=out_specs, check_vma=False)
```

```python
import functools

import jax
import jax.numpy as jnp
from jax import lax
from jax.experimental import pallas as pl
from jax.experimental.pallas import tpu as pltpu
from jax.sharding import PartitionSpec as P

CAP = 4
FIELDS = 4
STEP = 0.3
EPS4 = 4e-06
LANES = 128
DEEP = 16
THIN = 8
MESH = pl.DeviceIdType.MESH
EXACT = lax.Precision.HIGHEST


def one_sided(speed, lower, upper, s_m2, s_m1, s_0, s_p1, s_p2):
    ahead = speed > 0
    c = jnp.where(ahead, lower, upper)
    p = jnp.where(ahead, s_m2, s_p2)
    q = jnp.where(ahead, s_m1, s_p1)
    r = s_0
    w = jnp.where(ahead, s_p1, s_m1)
    k = 13.0 / 3.0
    a1, b1 = p - q, p - 3.0 * q
    a2, b2 = q - r, q + r
    a3, b3 = r - w, 3.0 * r - w
    t1 = k * (a1 * a1) + (b1 * b1 + EPS4)
    t2 = k * (a2 * a2) + (b2 * b2 + EPS4)
    t3 = k * (a3 * a3) + (b3 * b3 + EPS4)
    m1, m2, m3 = t2 * t3, t1 * t3, t1 * t2
    w1 = m1 * m1
    w2 = 6.0 * (m2 * m2)
    w3 = 3.0 * (m3 * m3)
    top = w1 * (2.0 * p - 5.0 * q) - w2 * (q + 2.0 * r) + w3 * (w - 4.0 * r)
    bottom = w1 + w2 + w3
    return speed * c - (jnp.abs(speed) * (1.0 / 6.0)) * (top / bottom)


def step_term(field, row, u, v):
    window = field[pl.ds(pl.multiple_of(row - 8, 8), 24), :]
    taps = [pltpu.roll(window, (24 - k) % 24, 0)[8:16] for k in range(-3, 4)]
    here = taps[3]
    width = here.shape[1]
    d = [taps[k + 1] - taps[k] for k in range(6)]
    s = [d[k + 1] - d[k] for k in range(5)]
    along_y = one_sided(v, d[2], d[3], *s)
    upper = pltpu.roll(here, width - 1, 1) - here
    lower = here - pltpu.roll(here, 1, 1)
    mid = upper - lower
    along_x = one_sided(
        u,
        lower,
        upper,
        pltpu.roll(mid, 2, 1),
        pltpu.roll(mid, 1, 1),
        mid,
        pltpu.roll(mid, width - 1, 1),
        pltpu.roll(mid, width - 2, 1),
    )
    return here, -(along_x + along_y)


def kernel(
    nb,
    nx,
    level_hbm,
    flow_hbm,
    parts_hbm,
    escaped_hbm,
    home_ref,
    land_ref,
    dest_ref,
    count_ref,
    out_ref,
    moved_hbm,
    f0,
    flow,
    f1,
    f2,
    side,
    from_left,
    from_right,
    parts,
    escaped,
    packed,
    records,
    rec_same,
    rec_left,
    load_sem,
    halo_send,
    halo_recv,
    pay_send,
    pay_recv,
    rec_send,
    rec_recv,
    left_send,
    left_recv,
    own_sem,
):
    g = lax.axis_index("gy")
    s = lax.axis_index("gx")
    height, across = level_hbm.shape
    width = across + LANES
    total = parts_hbm.shape[1]
    up = lax.rem(g + nb - 1, nb)
    down = lax.rem(g + 1, nb)
    left = lax.rem(s + nx - 1, nx)
    right = lax.rem(s + 1, nx)

    barrier = pltpu.get_barrier_semaphore()
    offsets = sorted({0, 1 % nx, (nx - 1) % nx})
    for off in offsets:
        strip = lax.rem(s + off, nx)

        def greet(k, carry, strip=strip):
            pl.semaphore_signal(
                barrier, inc=1, device_id=(lax.rem(g + k, nb), strip), device_id_type=MESH
            )
            return carry

        lax.fori_loop(1 if off == 0 else 0, nb, greet, 0)

    loads = [
        pltpu.make_async_copy(
            level_hbm, f0.at[pl.ds(DEEP, height), pl.ds(0, across)], load_sem.at[0]
        ),
        pltpu.make_async_copy(
            flow_hbm, flow.at[:, pl.ds(THIN, height), pl.ds(0, across)], load_sem.at[1]
        ),
        pltpu.make_async_copy(parts_hbm, parts, load_sem.at[2]),
        pltpu.make_async_copy(escaped_hbm, escaped, load_sem.at[3]),
    ]
    for copy in loads:
        copy.start()

    home = home_ref[...].reshape(1, total)
    land = land_ref[...].reshape(1, total)
    dest = dest_ref[...].reshape(1, total)
    lane = lax.broadcasted_iota(jnp.int32, (total, total), 1)
    sub = lax.broadcasted_iota(jnp.int32, (total, total), 0)

    def upright(row):
        return jnp.sum(jnp.where(lane == sub, row, 0), axis=1, keepdims=True)

    dest_col = upright(dest)
    home_col = upright(home)
    land_col = upright(land)
    live = count_ref[0]
    earlier = (dest == dest_col) & (sub < lane) & (sub < live)
    rank = jnp.sum(earlier.astype(jnp.int32), axis=0, keepdims=True)
    is_live = lax.broadcasted_iota(jnp.int32, (1, total), 1) < live
    slot = jnp.where(is_live, dest * (CAP * FIELDS) + rank * FIELDS, -64)
    own_row = jnp.where(is_live, dest * (2 * CAP) + rank, -64)
    next_band = jnp.where(dest == nb - 1, 0, dest + 1)
    past_row = jnp.where(is_live, next_band * (2 * CAP) + CAP + rank, -64)

    loads[0].wait()
    loads[1].wait()

    spot = lax.broadcasted_iota(jnp.int32, (height, LANES), 1)
    low = [
        f0[pl.ds(DEEP, height), 0:LANES],
        pltpu.roll(flow[0, pl.ds(THIN, height), 0:LANES], 16, 1),
        pltpu.roll(flow[1, pl.ds(THIN, height), 0:LANES], 32, 1),
    ]
    tail = pl.ds(across - LANES, LANES)
    high = [
        f0[pl.ds(DEEP, height), tail],
        pltpu.roll(flow[0, pl.ds(THIN, height), tail], LANES - 16, 1),
        pltpu.roll(flow[1, pl.ds(THIN, height), tail], LANES - 32, 1),
    ]
    low_edge = jnp.where(spot < 16, low[0], jnp.where(spot < 32, low[1], low[2]))
    high_edge = jnp.where(spot >= 112, high[0], jnp.where(spot >= 96, high[1], high[2]))
    side[...] = jnp.where(spot < 64, low_edge, high_edge)

    pl.semaphore_wait(barrier, nb * len(offsets) - 1)

    halo = []

    def send(src, dst, band, strip):
        i = len(halo)
        copy = pltpu.make_async_remote_copy(
            src_ref=src,
            dst_ref=dst,
            send_sem=halo_send.at[i],
            recv_sem=halo_recv.at[i],
            device_id=(band, strip),
            device_id_type=MESH,
        )
        copy.start()
        halo.append(copy)

    wide = pl.ds(0, across)
    for box, strip in ((from_right, left), (from_left, right))[: 2 if nx > 2 else 1]:
        send(side, box.at[pl.ds(DEEP, height)], g, strip)
        send(side.at[pl.ds(0, DEEP)], box.at[pl.ds(DEEP + height, DEEP)], up, strip)
        send(side.at[pl.ds(height - DEEP, DEEP)], box.at[pl.ds(0, DEEP)], down, strip)
    send(
        flow_hbm.at[:, pl.ds(0, THIN)], flow.at[:, pl.ds(THIN + height, THIN), wide], up, s
    )
    send(
        flow_hbm.at[:, pl.ds(height - THIN, THIN)], flow.at[:, pl.ds(0, THIN), wide], down, s
    )
    send(level_hbm.at[pl.ds(0, DEEP)], f0.at[pl.ds(DEEP + height, DEEP), wide], up, s)
    send(level_hbm.at[pl.ds(height - DEEP, DEEP)], f0.at[pl.ds(0, DEEP), wide], down, s)

    loads[2].wait()
    loads[3].wait()
    radius = parts[2]
    weight = escaped[...].astype(jnp.float32) * radius

    home_row = home_col // across
    home_at = home_col - home_row * across
    pick_lane = lax.broadcasted_iota(jnp.int32, (total, THIN + height), 1)
    pick_this = (pick_lane == home_row).astype(jnp.float32)
    pick_next = (pick_lane == home_row + 1).astype(jnp.float32)

    for copy in halo:
        copy.wait()

    spot = lax.broadcasted_iota(jnp.int32, (height + 2 * DEEP, LANES), 1)
    after = from_right[...]
    before = from_left[...] if nx > 2 else after
    end = pl.ds(across, LANES)
    f0[:, end] = jnp.where(spot < 64, after, before)
    inner = slice(DEEP - THIN, DEEP + height + THIN)
    spot, after, before = spot[inner], after[inner], before[inner]
    flow[0, :, end] = jnp.where(
        spot < 64, pltpu.roll(after, LANES - 16, 1), pltpu.roll(before, 16, 1)
    )
    flow[1, :, end] = jnp.where(
        spot < 64, pltpu.roll(after, LANES - 32, 1), pltpu.roll(before, 32, 1)
    )

    column = lax.broadcasted_iota(jnp.int32, (total, width), 1)
    this_column = column == home_at
    next_column = column == home_at + 1

    fraction_y = parts[1] + 0.5
    fraction_x = parts[0] + 0.5

    def mixture(component):
        cells = flow[component, pl.ds(THIN, height + THIN), :]
        this_row = jnp.dot(
            pick_this, cells, precision=EXACT, preferred_element_type=jnp.float32
        )
        next_row = jnp.dot(
            pick_next, cells, precision=EXACT, preferred_element_type=jnp.float32
        )

        def at(rows, mask):
            return jnp.sum(jnp.where(mask, rows, 0.0), axis=1, keepdims=True)

        return (
            (1.0 - fraction_y) * (1.0 - fraction_x) * at(this_row, this_column)
            + fraction_y * (1.0 - fraction_x) * at(next_row, this_column)
            + (1.0 - fraction_y) * fraction_x * at(this_row, next_column)
            + fraction_y * fraction_x * at(next_row, next_column)
        )

    new_x = parts[0] + STEP * mixture(0)
    new_y = parts[1] + STEP * mixture(1)

    slot_row = lax.broadcasted_iota(jnp.int32, (nb * CAP * FIELDS, total), 0)
    payload = None
    for k, rows in enumerate((new_x, new_y, radius, weight)):
        term = jnp.dot(
            (slot_row == slot + k).astype(jnp.float32),
            rows,
            precision=EXACT,
            preferred_element_type=jnp.float32,
        )
        payload = term if payload is None else payload + term
    packed[...] = payload

    gy = new_y + 0.5
    gx = new_x + 0.5

    def over(rows):
        return jnp.sum(rows, axis=1, keepdims=True)

    land_row = land_col // across
    columns = (
        land_row.astype(jnp.float32),
        (land_col - land_row * across).astype(jnp.float32),
        over(weight * (1.0 - gy) * (1.0 - gx)),
        over(weight * gy * (1.0 - gx)),
        over(weight * (1.0 - gy) * gx),
        over(weight * gy * gx),
    )
    spot = lax.broadcasted_iota(jnp.int32, (total, LANES), 1)
    table = jnp.zeros((total, LANES), jnp.float32)
    for k, one in enumerate(columns):
        table = jnp.where(spot == k, one, table)
    rec_row = lax.broadcasted_iota(jnp.int32, (nb * 2 * CAP, total), 0)
    records[...] = jnp.dot(
        ((rec_row == own_row) | (rec_row == past_row)).astype(jnp.float32),
        table,
        precision=EXACT,
        preferred_element_type=jnp.float32,
    )

    per = CAP * FIELDS
    two = 2 * CAP
    mine = pl.ds(pl.multiple_of(g * per, per), per)
    mine_rec = pl.ds(pl.multiple_of(g * two, two), two)

    def pay_copy(k):
        peer = lax.rem(g + k, nb)
        return pltpu.make_async_remote_copy(
            src_ref=packed.at[pl.ds(pl.multiple_of(peer * per, per), per)],
            dst_ref=moved_hbm.at[mine],
            send_sem=pay_send.at[k],
            recv_sem=pay_recv.at[k],
            device_id=(peer, s),
            device_id_type=MESH,
        )

    def rec_copy(k):
        peer = lax.rem(g + k, nb)
        return pltpu.make_async_remote_copy(
            src_ref=records.at[pl.ds(pl.multiple_of(peer * two, two), two)],
            dst_ref=rec_same.at[mine_rec],
            send_sem=rec_send.at[k],
            recv_sem=rec_recv.at[k],
            device_id=(peer, s),
            device_id_type=MESH,
        )

    def left_copy(k):
        peer = lax.rem(g + k, nb)
        return pltpu.make_async_remote_copy(
            src_ref=records.at[pl.ds(pl.multiple_of(peer * two, two), two)],
            dst_ref=rec_left.at[mine_rec],
            send_sem=left_send.at[k],
            recv_sem=left_recv.at[k],
            device_id=(peer, right),
            device_id_type=MESH,
        )

    def start_far(k, carry):
        rec_copy(k).start()
        left_copy(k).start()
        pay_copy(k).start()
        return carry

    left_copy(0).start()
    lax.fori_loop(1, nb, start_far, 0)
    own = [
        pltpu.make_async_copy(packed.at[mine], moved_hbm.at[mine], own_sem.at[0]),
        pltpu.make_async_copy(records.at[mine_rec], rec_same.at[mine_rec], own_sem.at[1]),
    ]
    for copy in own:
        copy.start()

    def first(i, carry):
        row = pl.multiple_of(i * 8, 8)
        here, term = step_term(
            f0, row + DEEP - THIN, flow[0, pl.ds(row, 8), :], flow[1, pl.ds(row, 8), :]
        )
        f1[pl.ds(row + DEEP - THIN, 8), :] = here + STEP * term
        return carry

    lax.fori_loop(0, (height + 2 * THIN) // 8, first, 0)

    def second(i, carry):
        row = pl.multiple_of(i * 8, 8)
        here, term = step_term(
            f1, row + DEEP - THIN, flow[0, pl.ds(row, 8), :], flow[1, pl.ds(row, 8), :]
        )
        at = pl.ds(row + DEEP - THIN, 8)
        f2[at, :] = 0.75 * f0[at, :] + 0.25 * (here + STEP * term)
        return carry

    lax.fori_loop(0, (height + 2 * THIN) // 8, second, 0)

    def third(i, carry):
        row = pl.multiple_of(i * 8, 8)
        at = pl.ds(row + THIN, 8)
        here, term = step_term(f2, row + DEEP, flow[0, at, :], flow[1, at, :])
        value = f0[pl.ds(row + DEEP, 8), :] / 3.0 + 2.0 / 3.0 * (here + STEP * term)
        out_ref[pl.ds(row, 8), :] = value[:, :across]
        return carry

    lax.fori_loop(0, height // 8, third, 0)

    for copy in own:
        copy.wait()
    left_copy(0).wait()

    def finish_far(k, carry):
        rec_copy(k).wait()
        left_copy(k).wait()
        return carry

    lax.fori_loop(1, nb, finish_far, 0)

    count = nb * two
    row_lane = lax.broadcasted_iota(jnp.int32, (count, LANES), 1)
    which = lax.broadcasted_iota(jnp.int32, (count, 1), 0)
    shift = jnp.where(lax.rem(which, two) >= CAP, float(height), 0.0)
    row_lane = row_lane.astype(jnp.float32)
    lane_out = lax.broadcasted_iota(jnp.int32, (count, across), 1).astype(jnp.float32)

    def laid(hot, rows):
        return lax.dot_general(
            hot.astype(jnp.float32),
            rows,
            (((0,), (0,)), ((), ())),
            precision=EXACT,
            preferred_element_type=jnp.float32,
        )[:height]

    box = rec_same[...]
    row_of = box[:, 0:1] - shift
    col_of = box[:, 1:2]
    at_col = lane_out == col_of
    at_next = lane_out == col_of + 1.0
    same_low = jnp.where(at_col, box[:, 2:3], jnp.where(at_next, box[:, 4:5], 0.0))
    same_high = jnp.where(at_col, box[:, 3:4], jnp.where(at_next, box[:, 5:6], 0.0))
    out_ref[...] += laid(row_lane == row_of, same_low) + laid(
        row_lane == row_of + 1.0, same_high
    )
    box = rec_left[...]
    row_of = box[:, 0:1] - shift
    spill = (box[:, 1:2] == float(across - 1)) & (row_lane == 0.0)
    left_low = jnp.where(spill, box[:, 4:5], 0.0)
    left_high = jnp.where(spill, box[:, 5:6], 0.0)
    out_ref[:, 0:LANES] += laid(row_lane == row_of, left_low) + laid(
        row_lane == row_of + 1.0, left_high
    )

    def finish_pay(k, carry):
        pay_copy(k).wait()
        return carry

    lax.fori_loop(1, nb, finish_pay, 0)


def shards(nb, nx, level_set, velocity, particles, escaped, home, land, dest, count):
    height, across = level_set.shape
    total, kinds, per_block = particles.shape
    width = across + LANES
    rows = nb * CAP * FIELDS
    recs = nb * 2 * CAP
    halos = 10 if nx > 2 else 7
    anywhere = pl.BlockSpec(memory_space=pl.ANY)
    vmem = pl.BlockSpec(memory_space=pltpu.VMEM)
    smem = pl.BlockSpec(memory_space=pltpu.SMEM)
    f32 = jnp.float32
    dma = pltpu.SemaphoreType.DMA
    level, moved = pl.pallas_call(
        functools.partial(kernel, nb, nx),
        out_shape=(
            pltpu.VMEM((height, across), f32),
            pltpu.VMEM((rows, per_block), f32),
        ),
        in_specs=[anywhere] * 4 + [vmem] * 3 + [smem],
        out_specs=(vmem, vmem),
        scratch_shapes=[
            pltpu.VMEM((height + 2 * DEEP, width), f32),
            pltpu.VMEM((2, height + 2 * THIN, width), f32),
            pltpu.VMEM((height + 2 * DEEP, width), f32),
            pltpu.VMEM((height + 2 * DEEP, width), f32),
            pltpu.VMEM((height, LANES), f32),
            pltpu.VMEM((height + 2 * DEEP, LANES), f32),
            pltpu.VMEM((height + 2 * DEEP, LANES), f32),
            pltpu.VMEM((kinds, total, per_block), f32),
            pltpu.VMEM(escaped.shape, jnp.int32),
            pltpu.VMEM((rows, per_block), f32),
            pltpu.VMEM((recs, LANES), f32),
            pltpu.VMEM((recs, LANES), f32),
            pltpu.VMEM((recs, LANES), f32),
            dma((4,)),
            dma((halos,)),
            dma((halos,)),
            dma((nb,)),
            dma((nb,)),
            dma((nb,)),
            dma((nb,)),
            dma((nb,)),
            dma((nb,)),
            dma((2,)),
        ],
        compiler_params=pltpu.CompilerParams(collective_id=0, has_side_effects=True),
    )(
        level_set,
        velocity,
        jnp.transpose(particles, (1, 0, 2)),
        escaped,
        home,
        land,
        dest,
        count,
    )
    return level, moved.reshape(nb * CAP, FIELDS, per_block)


def solution(mesh):
    in_specs = (
        P("gy", "gx"),
        P(None, "gy", "gx"),
        P(("gy", "gx"), None, None),
        P(("gy", "gx"), None),
        P(("gy", "gx")),
        P(("gy", "gx")),
        P(("gy", "gx")),
        P(("gy", "gx")),
    )
    out_specs = (P("gy", "gx"), P(("gy", "gx"), None, None))
    body = functools.partial(shards, mesh.shape["gy"], mesh.shape["gx"])
    return jax.shard_map(body, mesh=mesh, in_specs=in_specs, out_specs=out_specs, check_vma=False)
```

```python
import functools

import jax
import jax.numpy as jnp
from jax import lax
from jax.experimental import pallas as pl
from jax.experimental.pallas import tpu as pltpu
from jax.sharding import PartitionSpec as P

CAP = 4
FIELDS = 4
STEP = 0.3
EPS4 = 4e-06
LANES = 128
DEEP = 16
THIN = 8
MESH = pl.DeviceIdType.MESH


def one_sided(speed, lower, upper, s_m2, s_m1, s_0, s_p1, s_p2):
    ahead = speed > 0
    c = jnp.where(ahead, lower, upper)
    p = jnp.where(ahead, s_m2, s_p2)
    q = jnp.where(ahead, s_m1, s_p1)
    r = s_0
    w = jnp.where(ahead, s_p1, s_m1)
    k = 13.0 / 3.0
    a1, b1 = p - q, p - 3.0 * q
    a2, b2 = q - r, q + r
    a3, b3 = r - w, 3.0 * r - w
    t1 = k * (a1 * a1) + (b1 * b1 + EPS4)
    t2 = k * (a2 * a2) + (b2 * b2 + EPS4)
    t3 = k * (a3 * a3) + (b3 * b3 + EPS4)
    m1, m2, m3 = t2 * t3, t1 * t3, t1 * t2
    w1 = m1 * m1
    w2 = 6.0 * (m2 * m2)
    w3 = 3.0 * (m3 * m3)
    top = w1 * (2.0 * p - 5.0 * q) - w2 * (q + 2.0 * r) + w3 * (w - 4.0 * r)
    bottom = w1 + w2 + w3
    return speed * c - (jnp.abs(speed) * (1.0 / 6.0)) * (top / bottom)


def step_term(field, row, u, v):
    window = field[pl.ds(pl.multiple_of(row - 8, 8), 24), :]
    taps = [pltpu.roll(window, (24 - k) % 24, 0)[8:16] for k in range(-3, 4)]
    here = taps[3]
    width = here.shape[1]
    d = [taps[k + 1] - taps[k] for k in range(6)]
    s = [d[k + 1] - d[k] for k in range(5)]
    along_y = one_sided(v, d[2], d[3], *s)
    upper = pltpu.roll(here, width - 1, 1) - here
    lower = here - pltpu.roll(here, 1, 1)
    mid = upper - lower
    along_x = one_sided(
        u,
        lower,
        upper,
        pltpu.roll(mid, 2, 1),
        pltpu.roll(mid, 1, 1),
        mid,
        pltpu.roll(mid, width - 1, 1),
        pltpu.roll(mid, width - 2, 1),
    )
    return here, -(along_x + along_y)


def pieces(x):
    top = x.astype(jnp.bfloat16)
    rest = x - top.astype(jnp.float32)
    middle = rest.astype(jnp.bfloat16)
    return top, middle, (rest - middle.astype(jnp.float32)).astype(jnp.bfloat16)


def chosen(hot, x):
    hot = hot.astype(jnp.bfloat16)
    top, middle, last = (
        jnp.dot(hot, part, preferred_element_type=jnp.float32) for part in pieces(x)
    )
    return top + (middle + last)


def kernel(
    nb,
    nx,
    level_hbm,
    flow_hbm,
    parts_hbm,
    escaped_hbm,
    home_hbm,
    land_hbm,
    dest_hbm,
    count_hbm,
    out_ref,
    moved_hbm,
    f0,
    flow,
    f1,
    f2,
    side,
    from_left,
    from_right,
    parts,
    escaped,
    home_ref,
    land_ref,
    dest_ref,
    count_ref,
    packed,
    records,
    rec_same,
    rec_left,
    load_sem,
    halo_send,
    halo_recv,
    pay_send,
    pay_recv,
    rec_send,
    rec_recv,
    left_send,
    left_recv,
    own_sem,
):
    g = lax.axis_index("gy")
    s = lax.axis_index("gx")
    height, across = level_hbm.shape
    width = across + LANES
    total = parts_hbm.shape[1]
    up = lax.rem(g + nb - 1, nb)
    down = lax.rem(g + 1, nb)
    left = lax.rem(s + nx - 1, nx)
    right = lax.rem(s + 1, nx)

    barrier = pltpu.get_barrier_semaphore()
    offsets = sorted({0, 1 % nx, (nx - 1) % nx})
    for off in offsets:
        strip = lax.rem(s + off, nx)

        def greet(k, carry, strip=strip):
            pl.semaphore_signal(
                barrier, inc=1, device_id=(lax.rem(g + k, nb), strip), device_id_type=MESH
            )
            return carry

        lax.fori_loop(1 if off == 0 else 0, nb, greet, 0)

    loads = [
        pltpu.make_async_copy(
            level_hbm, f0.at[pl.ds(DEEP, height), pl.ds(0, across)], load_sem.at[0]
        ),
        pltpu.make_async_copy(
            flow_hbm, flow.at[:, pl.ds(THIN, height), pl.ds(0, across)], load_sem.at[1]
        ),
        pltpu.make_async_copy(parts_hbm, parts, load_sem.at[2]),
        pltpu.make_async_copy(escaped_hbm, escaped, load_sem.at[3]),
    ]
    small = [
        pltpu.make_async_copy(src, dst, load_sem.at[4 + k])
        for k, (src, dst) in enumerate(
            (
                (home_hbm, home_ref),
                (land_hbm, land_ref),
                (dest_hbm, dest_ref),
                (count_hbm, count_ref),
            )
        )
    ]
    for copy in small + loads:
        copy.start()
    for copy in small:
        copy.wait()

    home = home_ref[...].reshape(1, total)
    land = land_ref[...].reshape(1, total)
    dest = dest_ref[...].reshape(1, total)
    lane = lax.broadcasted_iota(jnp.int32, (total, total), 1)
    sub = lax.broadcasted_iota(jnp.int32, (total, total), 0)

    def upright(row):
        return jnp.sum(jnp.where(lane == sub, row, 0), axis=1, keepdims=True)

    dest_col = upright(dest)
    home_col = upright(home)
    land_col = upright(land)
    live = count_ref[0]
    earlier = (dest == dest_col) & (sub < lane) & (sub < live)
    rank = jnp.sum(earlier.astype(jnp.int32), axis=0, keepdims=True)
    is_live = lax.broadcasted_iota(jnp.int32, (1, total), 1) < live
    slot = jnp.where(is_live, dest * CAP + rank, -1)
    rank_col = upright(rank)
    own_band = jnp.where(is_live, dest, -1)
    past_band = jnp.where(is_live, jnp.where(dest == nb - 1, 0, dest + 1), -1)

    loads[0].wait()
    loads[1].wait()

    spot = lax.broadcasted_iota(jnp.int32, (height, LANES), 1)
    low = [
        f0[pl.ds(DEEP, height), 0:LANES],
        pltpu.roll(flow[0, pl.ds(THIN, height), 0:LANES], 16, 1),
        pltpu.roll(flow[1, pl.ds(THIN, height), 0:LANES], 32, 1),
    ]
    tail = pl.ds(across - LANES, LANES)
    high = [
        f0[pl.ds(DEEP, height), tail],
        pltpu.roll(flow[0, pl.ds(THIN, height), tail], LANES - 16, 1),
        pltpu.roll(flow[1, pl.ds(THIN, height), tail], LANES - 32, 1),
    ]
    low_edge = jnp.where(spot < 16, low[0], jnp.where(spot < 32, low[1], low[2]))
    high_edge = jnp.where(spot >= 112, high[0], jnp.where(spot >= 96, high[1], high[2]))
    side[...] = jnp.where(spot < 64, low_edge, high_edge)

    pl.semaphore_wait(barrier, nb * len(offsets) - 1)

    halo = []

    def send(src, dst, band, strip):
        i = len(halo)
        copy = pltpu.make_async_remote_copy(
            src_ref=src,
            dst_ref=dst,
            send_sem=halo_send.at[i],
            recv_sem=halo_recv.at[i],
            device_id=(band, strip),
            device_id_type=MESH,
        )
        copy.start()
        halo.append(copy)

    wide = pl.ds(0, across)
    for box, strip in ((from_right, left), (from_left, right))[: 2 if nx > 2 else 1]:
        send(side, box.at[pl.ds(DEEP, height)], g, strip)
        send(side.at[pl.ds(0, DEEP)], box.at[pl.ds(DEEP + height, DEEP)], up, strip)
        send(side.at[pl.ds(height - DEEP, DEEP)], box.at[pl.ds(0, DEEP)], down, strip)
    send(
        flow_hbm.at[:, pl.ds(0, THIN)], flow.at[:, pl.ds(THIN + height, THIN), wide], up, s
    )
    send(
        flow_hbm.at[:, pl.ds(height - THIN, THIN)], flow.at[:, pl.ds(0, THIN), wide], down, s
    )
    send(level_hbm.at[pl.ds(0, DEEP)], f0.at[pl.ds(DEEP + height, DEEP), wide], up, s)
    send(level_hbm.at[pl.ds(height - DEEP, DEEP)], f0.at[pl.ds(0, DEEP), wide], down, s)

    loads[2].wait()
    loads[3].wait()
    radius = parts[2]
    weight = escaped[...].astype(jnp.float32) * radius

    home_row = home_col // across
    home_at = home_col - home_row * across
    pick_lane = lax.broadcasted_iota(jnp.int32, (total, THIN + height), 1)
    pick = jnp.concatenate(
        [
            (pick_lane == home_row).astype(jnp.float32),
            (pick_lane == home_row + 1).astype(jnp.float32),
        ],
        axis=0,
    )
    slot_row = lax.broadcasted_iota(jnp.int32, (nb * CAP, total), 0)
    slot_hot = (slot_row == slot).astype(jnp.float32)
    band_row = lax.broadcasted_iota(jnp.int32, (nb, total), 0)
    own_hot = (band_row == own_band).astype(jnp.float32)
    past_hot = (band_row == past_band).astype(jnp.float32)
    land_row = land_col // across

    for copy in halo[:-2]:
        copy.wait()

    spot = lax.broadcasted_iota(jnp.int32, (height + 2 * DEEP, LANES), 1)
    after = from_right[...]
    before = from_left[...] if nx > 2 else after
    end = pl.ds(across, LANES)
    f0[:, end] = jnp.where(spot < 64, after, before)
    inner = slice(DEEP - THIN, DEEP + height + THIN)
    spot, after, before = spot[inner], after[inner], before[inner]
    flow[0, :, end] = jnp.where(
        spot < 64, pltpu.roll(after, LANES - 16, 1), pltpu.roll(before, 16, 1)
    )
    flow[1, :, end] = jnp.where(
        spot < 64, pltpu.roll(after, LANES - 32, 1), pltpu.roll(before, 32, 1)
    )

    column = lax.broadcasted_iota(jnp.int32, (total, width), 1)
    this_column = column == home_at
    next_column = column == home_at + 1

    fraction_y = parts[1] + 0.5
    fraction_x = parts[0] + 0.5

    def mixture(component):
        cells = flow[component, pl.ds(THIN, height + THIN), :]
        both = chosen(pick, cells)
        this_row, next_row = both[:total], both[total:]

        def at(rows, mask):
            return jnp.sum(jnp.where(mask, rows, 0.0), axis=1, keepdims=True)

        return (
            (1.0 - fraction_y) * (1.0 - fraction_x) * at(this_row, this_column)
            + fraction_y * (1.0 - fraction_x) * at(next_row, this_column)
            + (1.0 - fraction_y) * fraction_x * at(this_row, next_column)
            + fraction_y * fraction_x * at(next_row, next_column)
        )

    new_x = parts[0] + STEP * mixture(0)
    new_y = parts[1] + STEP * mixture(1)

    payload = chosen(slot_hot, jnp.concatenate([new_x, new_y, radius, weight], axis=1))
    for k in range(FIELDS):
        packed[pl.ds(k, nb * CAP, stride=FIELDS), :] = payload[:, k * LANES : (k + 1) * LANES]

    gy = new_y + 0.5
    gx = new_x + 0.5

    def over(rows):
        return jnp.sum(rows, axis=1, keepdims=True)

    columns = (
        land_row.astype(jnp.float32),
        (land_col - land_row * across).astype(jnp.float32),
        over(weight * (1.0 - gy) * (1.0 - gx)),
        over(weight * gy * (1.0 - gx)),
        over(weight * (1.0 - gy) * gx),
        over(weight * gy * gx),
    )
    spot = lax.broadcasted_iota(jnp.int32, (total, LANES), 1)
    table = jnp.zeros((total, LANES), jnp.float32)
    for k, one in enumerate(columns):
        table = jnp.where(spot // (2 * CAP) == k, one, table)
    place = spot % (2 * CAP)
    sheet = chosen(own_hot, jnp.where(place == rank_col, table, 0.0)) + chosen(
        past_hot, jnp.where(place == rank_col + CAP, table, 0.0)
    )
    for band in range(nb):
        records[band] = sheet[band : band + 1]

    per = CAP * FIELDS
    mine = pl.ds(pl.multiple_of(g * per, per), per)

    def pay_copy(k):
        peer = lax.rem(g + k, nb)
        return pltpu.make_async_remote_copy(
            src_ref=packed.at[pl.ds(pl.multiple_of(peer * per, per), per)],
            dst_ref=moved_hbm.at[mine],
            send_sem=pay_send.at[k],
            recv_sem=pay_recv.at[k],
            device_id=(peer, s),
            device_id_type=MESH,
        )

    def rec_copy(k):
        peer = lax.rem(g + k, nb)
        return pltpu.make_async_remote_copy(
            src_ref=records.at[peer],
            dst_ref=rec_same.at[g],
            send_sem=rec_send.at[k],
            recv_sem=rec_recv.at[k],
            device_id=(peer, s),
            device_id_type=MESH,
        )

    def left_copy(k):
        peer = lax.rem(g + k, nb)
        return pltpu.make_async_remote_copy(
            src_ref=records.at[peer],
            dst_ref=rec_left.at[g],
            send_sem=left_send.at[k],
            recv_sem=left_recv.at[k],
            device_id=(peer, right),
            device_id_type=MESH,
        )

    def start_far(k, carry):
        rec_copy(k).start()
        left_copy(k).start()
        pay_copy(k).start()
        return carry

    left_copy(0).start()
    lax.fori_loop(1, nb, start_far, 0)
    own = [
        pltpu.make_async_copy(packed.at[mine], moved_hbm.at[mine], own_sem.at[0]),
        pltpu.make_async_copy(records.at[g], rec_same.at[g], own_sem.at[1]),
    ]
    for copy in own:
        copy.start()

    for copy in halo[-2:]:
        copy.wait()

    def first(i, carry):
        row = pl.multiple_of(i * 8, 8)
        here, term = step_term(
            f0, row + DEEP - THIN, flow[0, pl.ds(row, 8), :], flow[1, pl.ds(row, 8), :]
        )
        f1[pl.ds(row + DEEP - THIN, 8), :] = here + STEP * term
        return carry

    lax.fori_loop(0, (height + 2 * THIN) // 8, first, 0)

    def second(i, carry):
        row = pl.multiple_of(i * 8, 8)
        here, term = step_term(
            f1, row + DEEP - THIN, flow[0, pl.ds(row, 8), :], flow[1, pl.ds(row, 8), :]
        )
        at = pl.ds(row + DEEP - THIN, 8)
        f2[at, :] = 0.75 * f0[at, :] + 0.25 * (here + STEP * term)
        return carry

    lax.fori_loop(0, (height + 2 * THIN) // 8, second, 0)

    def third(i, carry):
        row = pl.multiple_of(i * 8, 8)
        at = pl.ds(row + THIN, 8)
        here, term = step_term(f2, row + DEEP, flow[0, at, :], flow[1, at, :])
        value = f0[pl.ds(row + DEEP, 8), :] / 3.0 + 2.0 / 3.0 * (here + STEP * term)
        out_ref[pl.ds(row, 8), :] = value[:, :across]
        return carry

    lax.fori_loop(0, height // 8, third, 0)

    for copy in own:
        copy.wait()
    left_copy(0).wait()

    def finish_far(k, carry):
        rec_copy(k).wait()
        left_copy(k).wait()
        return carry

    lax.fori_loop(1, nb, finish_far, 0)

    row_lane = lax.broadcasted_iota(jnp.int32, (nb, LANES), 1).astype(jnp.float32)
    lane_out = lax.broadcasted_iota(jnp.int32, (nb, across), 1).astype(jnp.float32)
    spread = 2 * CAP

    def slots_of(box):
        for j in range(spread):
            fields = [box[:, k * spread + j : k * spread + j + 1] for k in range(6)]
            if j >= CAP:
                fields[0] = fields[0] - float(height)
            yield fields

    def laid(hots, rows):
        hot = jnp.transpose(jnp.concatenate(hots, axis=0))[:height]
        return chosen(hot, jnp.concatenate(rows, axis=0))

    hots, rows = [], []
    for row, col, low_low, high_low, low_high, high_high in slots_of(
        jnp.concatenate([rec_same[k] for k in range(nb)], axis=0)
    ):
        here, beside = lane_out == col, lane_out == col + 1.0
        hots += [(row_lane == row).astype(jnp.float32), (row_lane == row + 1.0).astype(jnp.float32)]
        rows += [
            jnp.where(here, low_low, jnp.where(beside, low_high, 0.0)),
            jnp.where(here, high_low, jnp.where(beside, high_high, 0.0)),
        ]
    out_ref[...] += laid(hots, rows)
    hots, rows = [], []
    for row, col, low_low, high_low, low_high, high_high in slots_of(
        jnp.concatenate([rec_left[k] for k in range(nb)], axis=0)
    ):
        spill = (col == float(across - 1)) & (row_lane == 0.0)
        hots += [(row_lane == row).astype(jnp.float32), (row_lane == row + 1.0).astype(jnp.float32)]
        rows += [jnp.where(spill, low_high, 0.0), jnp.where(spill, high_high, 0.0)]
    out_ref[:, 0:LANES] += laid(hots, rows)

    def finish_pay(k, carry):
        pay_copy(k).wait()
        return carry

    lax.fori_loop(1, nb, finish_pay, 0)


def shards(nb, nx, level_set, velocity, particles, escaped, home, land, dest, count):
    height, across = level_set.shape
    total, kinds, per_block = particles.shape
    width = across + LANES
    rows = nb * CAP * FIELDS
    halos = 10 if nx > 2 else 7
    vmem = pl.BlockSpec(memory_space=pltpu.VMEM)
    f32 = jnp.float32
    dma = pltpu.SemaphoreType.DMA
    level, moved = pl.pallas_call(
        functools.partial(kernel, nb, nx),
        out_shape=(
            pltpu.VMEM((height, across), f32),
            pltpu.VMEM((rows, per_block), f32),
        ),
        in_specs=[pl.BlockSpec(memory_space=pltpu.HBM)] * 8,
        out_specs=(vmem, vmem),
        scratch_shapes=[
            pltpu.VMEM((height + 2 * DEEP, width), f32),
            pltpu.VMEM((2, height + 2 * THIN, width), f32),
            pltpu.VMEM((height + 2 * DEEP, width), f32),
            pltpu.VMEM((height + 2 * DEEP, width), f32),
            pltpu.VMEM((height, LANES), f32),
            pltpu.VMEM((height + 2 * DEEP, LANES), f32),
            pltpu.VMEM((height + 2 * DEEP, LANES), f32),
            pltpu.VMEM((kinds, total, per_block), f32),
            pltpu.VMEM(escaped.shape, jnp.int32),
            pltpu.VMEM(home.shape, jnp.int32),
            pltpu.VMEM(land.shape, jnp.int32),
            pltpu.VMEM(dest.shape, jnp.int32),
            pltpu.SMEM(count.shape, jnp.int32),
            pltpu.VMEM((rows, per_block), f32),
            pltpu.VMEM((nb, 1, LANES), f32),
            pltpu.VMEM((nb, 1, LANES), f32),
            pltpu.VMEM((nb, 1, LANES), f32),
            dma((8,)),
            dma((halos,)),
            dma((halos,)),
            dma((nb,)),
            dma((nb,)),
            dma((nb,)),
            dma((nb,)),
            dma((nb,)),
            dma((nb,)),
            dma((2,)),
        ],
        compiler_params=pltpu.CompilerParams(collective_id=0, has_side_effects=True),
    )(
        level_set,
        velocity,
        jnp.transpose(particles, (1, 0, 2)),
        escaped,
        home,
        land,
        dest,
        count,
    )
    return level, moved.reshape(nb * CAP, FIELDS, per_block)


def solution(mesh):
    in_specs = (
        P("gy", "gx"),
        P(None, "gy", "gx"),
        P(("gy", "gx"), None, None),
        P(("gy", "gx"), None),
        P(("gy", "gx")),
        P(("gy", "gx")),
        P(("gy", "gx")),
        P(("gy", "gx")),
    )
    out_specs = (P("gy", "gx"), P(("gy", "gx"), None, None))
    body = functools.partial(shards, mesh.shape["gy"], mesh.shape["gx"])
    return jax.shard_map(body, mesh=mesh, in_specs=in_specs, out_specs=out_specs, check_vma=False)
```

```python
import functools

import jax
import jax.numpy as jnp
from jax import lax
from jax.experimental import pallas as pl
from jax.experimental.pallas import tpu as pltpu
from jax.sharding import PartitionSpec as P

CAP = 4
FIELDS = 4
STEP = 0.3
EPS4 = 4e-06
LANES = 128
DEEP = 16
THIN = 8
MESH = pl.DeviceIdType.MESH


def one_sided(speed, lower, upper, s_m2, s_m1, s_0, s_p1, s_p2):
    ahead = speed > 0
    c = jnp.where(ahead, lower, upper)
    p = jnp.where(ahead, s_m2, s_p2)
    q = jnp.where(ahead, s_m1, s_p1)
    r = s_0
    w = jnp.where(ahead, s_p1, s_m1)
    k = 13.0 / 3.0
    a1, b1 = p - q, p - 3.0 * q
    a2, b2 = q - r, q + r
    a3, b3 = r - w, 3.0 * r - w
    t1 = k * (a1 * a1) + (b1 * b1 + EPS4)
    t2 = k * (a2 * a2) + (b2 * b2 + EPS4)
    t3 = k * (a3 * a3) + (b3 * b3 + EPS4)
    m1, m2, m3 = t2 * t3, t1 * t3, t1 * t2
    w1 = m1 * m1
    w2 = 6.0 * (m2 * m2)
    w3 = 3.0 * (m3 * m3)
    top = w1 * (2.0 * p - 5.0 * q) - w2 * (q + 2.0 * r) + w3 * (w - 4.0 * r)
    bottom = w1 + w2 + w3
    return speed * c - (jnp.abs(speed) * (1.0 / 6.0)) * (top / bottom)


def row_term(field, row, lanes, v):
    window = field[pl.ds(pl.multiple_of(row - 8, 8), 24), lanes]
    taps = [pltpu.roll(window, (24 - k) % 24, 0)[8:16] for k in range(-3, 4)]
    d = [taps[k + 1] - taps[k] for k in range(6)]
    s = [d[k + 1] - d[k] for k in range(5)]
    return one_sided(v, d[2], d[3], *s)


def column_term(here, u):
    width = here.shape[1]
    upper = pltpu.roll(here, width - 1, 1) - here
    lower = here - pltpu.roll(here, 1, 1)
    mid = upper - lower
    return one_sided(
        u,
        lower,
        upper,
        pltpu.roll(mid, 2, 1),
        pltpu.roll(mid, 1, 1),
        mid,
        pltpu.roll(mid, width - 1, 1),
        pltpu.roll(mid, width - 2, 1),
    )


def step_term(field, row, u, v):
    here = field[pl.ds(pl.multiple_of(row, 8), 8), :]
    return here, -(column_term(here, u) + row_term(field, row, slice(None), v))


def pieces(x):
    top = x.astype(jnp.bfloat16)
    rest = x - top.astype(jnp.float32)
    middle = rest.astype(jnp.bfloat16)
    return top, middle, (rest - middle.astype(jnp.float32)).astype(jnp.bfloat16)


def chosen(hot, x):
    hot = hot.astype(jnp.bfloat16)
    top, middle, last = (
        jnp.dot(hot, part, preferred_element_type=jnp.float32) for part in pieces(x)
    )
    return top + (middle + last)


def kernel(
    nb,
    nx,
    level_hbm,
    flow_hbm,
    parts_hbm,
    escaped_hbm,
    home_hbm,
    land_hbm,
    dest_hbm,
    count_hbm,
    out_ref,
    moved_hbm,
    f0,
    flow,
    f1,
    f2,
    side,
    from_left,
    from_right,
    parts,
    escaped,
    home_ref,
    land_ref,
    dest_ref,
    count_ref,
    packed,
    records,
    rec_same,
    rec_left,
    load_sem,
    halo_send,
    halo_recv,
    pay_send,
    pay_recv,
    rec_send,
    rec_recv,
    left_send,
    left_recv,
    own_sem,
):
    g = lax.axis_index("gy")
    s = lax.axis_index("gx")
    height, across = level_hbm.shape
    width = across + LANES
    total = parts_hbm.shape[1]
    up = lax.rem(g + nb - 1, nb)
    down = lax.rem(g + 1, nb)
    left = lax.rem(s + nx - 1, nx)
    right = lax.rem(s + 1, nx)

    barrier = pltpu.get_barrier_semaphore()
    offsets = sorted({0, 1 % nx, (nx - 1) % nx})
    for off in offsets:
        strip = lax.rem(s + off, nx)

        def greet(k, carry, strip=strip):
            pl.semaphore_signal(
                barrier, inc=1, device_id=(lax.rem(g + k, nb), strip), device_id_type=MESH
            )
            return carry

        lax.fori_loop(1 if off == 0 else 0, nb, greet, 0)

    loads = [
        pltpu.make_async_copy(
            level_hbm, f0.at[pl.ds(DEEP, height), pl.ds(0, across)], load_sem.at[0]
        ),
        pltpu.make_async_copy(
            flow_hbm, flow.at[:, pl.ds(THIN, height), pl.ds(0, across)], load_sem.at[1]
        ),
        pltpu.make_async_copy(parts_hbm, parts, load_sem.at[2]),
        pltpu.make_async_copy(escaped_hbm, escaped, load_sem.at[3]),
    ]
    small = [
        pltpu.make_async_copy(src, dst, load_sem.at[4 + k])
        for k, (src, dst) in enumerate(
            (
                (home_hbm, home_ref),
                (land_hbm, land_ref),
                (dest_hbm, dest_ref),
                (count_hbm, count_ref),
            )
        )
    ]
    for copy in small + loads:
        copy.start()
    for copy in small:
        copy.wait()

    home = home_ref[...].reshape(1, total)
    land = land_ref[...].reshape(1, total)
    dest = dest_ref[...].reshape(1, total)
    lane = lax.broadcasted_iota(jnp.int32, (total, total), 1)
    sub = lax.broadcasted_iota(jnp.int32, (total, total), 0)

    def upright(row):
        return jnp.sum(jnp.where(lane == sub, row, 0), axis=1, keepdims=True)

    dest_col = upright(dest)
    home_col = upright(home)
    land_col = upright(land)
    live = count_ref[0]
    earlier = (dest == dest_col) & (sub < lane) & (sub < live)
    rank = jnp.sum(earlier.astype(jnp.int32), axis=0, keepdims=True)
    is_live = lax.broadcasted_iota(jnp.int32, (1, total), 1) < live
    slot = jnp.where(is_live, dest * CAP + rank, -1)
    rank_col = upright(rank)
    own_band = jnp.where(is_live, dest, -1)
    past_band = jnp.where(is_live, jnp.where(dest == nb - 1, 0, dest + 1), -1)

    pl.semaphore_wait(barrier, nb * len(offsets) - 1)

    halo = []

    def send(src, dst, band, strip):
        i = len(halo)
        copy = pltpu.make_async_remote_copy(
            src_ref=src,
            dst_ref=dst,
            send_sem=halo_send.at[i],
            recv_sem=halo_recv.at[i],
            device_id=(band, strip),
            device_id_type=MESH,
        )
        copy.start()
        halo.append(copy)

    wide = pl.ds(0, across)
    send(
        flow_hbm.at[:, pl.ds(0, THIN)], flow.at[:, pl.ds(THIN + height, THIN), wide], up, s
    )
    send(
        flow_hbm.at[:, pl.ds(height - THIN, THIN)], flow.at[:, pl.ds(0, THIN), wide], down, s
    )
    send(level_hbm.at[pl.ds(0, DEEP)], f0.at[pl.ds(DEEP + height, DEEP), wide], up, s)
    send(level_hbm.at[pl.ds(height - DEEP, DEEP)], f0.at[pl.ds(0, DEEP), wide], down, s)

    loads[0].wait()
    loads[1].wait()

    spot = lax.broadcasted_iota(jnp.int32, (height, LANES), 1)
    low = [
        f0[pl.ds(DEEP, height), 0:LANES],
        pltpu.roll(flow[0, pl.ds(THIN, height), 0:LANES], 16, 1),
        pltpu.roll(flow[1, pl.ds(THIN, height), 0:LANES], 32, 1),
    ]
    tail = pl.ds(across - LANES, LANES)
    high = [
        f0[pl.ds(DEEP, height), tail],
        pltpu.roll(flow[0, pl.ds(THIN, height), tail], LANES - 16, 1),
        pltpu.roll(flow[1, pl.ds(THIN, height), tail], LANES - 32, 1),
    ]
    low_edge = jnp.where(spot < 16, low[0], jnp.where(spot < 32, low[1], low[2]))
    high_edge = jnp.where(spot >= 112, high[0], jnp.where(spot >= 96, high[1], high[2]))
    side[...] = jnp.where(spot < 64, low_edge, high_edge)

    for box, strip in ((from_right, left), (from_left, right))[: 2 if nx > 2 else 1]:
        send(side, box.at[pl.ds(DEEP, height)], g, strip)
        send(side.at[pl.ds(0, DEEP)], box.at[pl.ds(DEEP + height, DEEP)], up, strip)
        send(side.at[pl.ds(height - DEEP, DEEP)], box.at[pl.ds(0, DEEP)], down, strip)
    loads[2].wait()
    loads[3].wait()
    radius = parts[2]
    weight = escaped[...].astype(jnp.float32) * radius

    home_row = home_col // across
    home_at = home_col - home_row * across
    pick_lane = lax.broadcasted_iota(jnp.int32, (total, THIN + height), 1)
    pick = jnp.concatenate(
        [
            (pick_lane == home_row).astype(jnp.float32),
            (pick_lane == home_row + 1).astype(jnp.float32),
        ],
        axis=0,
    )
    slot_row = lax.broadcasted_iota(jnp.int32, (nb * CAP, total), 0)
    slot_hot = (slot_row == slot).astype(jnp.float32)
    band_row = lax.broadcasted_iota(jnp.int32, (nb, total), 0)
    own_hot = (band_row == own_band).astype(jnp.float32)
    past_hot = (band_row == past_band).astype(jnp.float32)
    land_row = land_col // across

    column = lax.broadcasted_iota(jnp.int32, (total, across), 1)
    this_column = column == home_at
    next_column = column == home_at + 1
    at_last = home_row == height - 1
    at_edge = home_at == across - 1
    fraction_y = parts[1] + 0.5
    fraction_x = parts[0] + 0.5

    def at(rows, mask):
        return jnp.sum(jnp.where(mask, rows, 0.0), axis=1, keepdims=True)

    inside = []
    for component in range(2):
        both = chosen(pick[:, :height], flow[component, pl.ds(THIN, height), wide])
        inside.append(
            [
                at(both[low : low + total], mask)
                for mask in (this_column, next_column)
                for low in (0, total)
            ]
        )

    def early(i, carry):
        row = pl.multiple_of(i * 8, 8)
        rows = pl.ds(row + DEEP - THIN, 8)
        f1[rows, wide] = row_term(f0, row + DEEP - THIN, wide, flow[1, pl.ds(row, 8), wide])
        return carry

    lax.fori_loop(2, height // 8, early, 0)

    for copy in halo[:2] + halo[4:]:
        copy.wait()

    spot = lax.broadcasted_iota(jnp.int32, (height + 2 * DEEP, LANES), 1)
    after = from_right[...]
    before = from_left[...] if nx > 2 else after
    end = pl.ds(across, LANES)
    f0[:, end] = jnp.where(spot < 64, after, before)
    inner = slice(DEEP - THIN, DEEP + height + THIN)
    spot, after, before = spot[inner], after[inner], before[inner]
    flow[0, :, end] = jnp.where(
        spot < 64, pltpu.roll(after, LANES - 16, 1), pltpu.roll(before, 16, 1)
    )
    flow[1, :, end] = jnp.where(
        spot < 64, pltpu.roll(after, LANES - 32, 1), pltpu.roll(before, 32, 1)
    )

    def mixture(component):
        low_low, high_low, low_high, high_high = inside[component]
        below = flow[component, pl.ds(THIN + height, THIN), wide][0:1]
        beyond = chosen(pick, flow[component, pl.ds(THIN, height + THIN), end])[:, 0:1]
        high_low = high_low + jnp.where(at_last, at(below, this_column), 0.0)
        high_high = high_high + jnp.where(at_last, at(below, next_column), 0.0)
        low_high = low_high + jnp.where(at_edge, beyond[:total], 0.0)
        high_high = high_high + jnp.where(at_edge, beyond[total:], 0.0)
        return (
            (1.0 - fraction_y) * (1.0 - fraction_x) * low_low
            + fraction_y * (1.0 - fraction_x) * high_low
            + (1.0 - fraction_y) * fraction_x * low_high
            + fraction_y * fraction_x * high_high
        )

    new_x = parts[0] + STEP * mixture(0)
    new_y = parts[1] + STEP * mixture(1)

    payload = chosen(slot_hot, jnp.concatenate([new_x, new_y, radius, weight], axis=1))
    for k in range(FIELDS):
        packed[pl.ds(k, nb * CAP, stride=FIELDS), :] = payload[:, k * LANES : (k + 1) * LANES]

    gy = new_y + 0.5
    gx = new_x + 0.5

    def over(rows):
        return jnp.sum(rows, axis=1, keepdims=True)

    columns = (
        land_row.astype(jnp.float32),
        (land_col - land_row * across).astype(jnp.float32),
        over(weight * (1.0 - gy) * (1.0 - gx)),
        over(weight * gy * (1.0 - gx)),
        over(weight * (1.0 - gy) * gx),
        over(weight * gy * gx),
    )
    spot = lax.broadcasted_iota(jnp.int32, (total, LANES), 1)
    table = jnp.zeros((total, LANES), jnp.float32)
    for k, one in enumerate(columns):
        table = jnp.where(spot // (2 * CAP) == k, one, table)
    place = spot % (2 * CAP)
    sheet = chosen(own_hot, jnp.where(place == rank_col, table, 0.0)) + chosen(
        past_hot, jnp.where(place == rank_col + CAP, table, 0.0)
    )
    for band in range(nb):
        records[band] = sheet[band : band + 1]

    per = CAP * FIELDS
    mine = pl.ds(pl.multiple_of(g * per, per), per)

    def pay_copy(k):
        peer = lax.rem(g + k, nb)
        return pltpu.make_async_remote_copy(
            src_ref=packed.at[pl.ds(pl.multiple_of(peer * per, per), per)],
            dst_ref=moved_hbm.at[mine],
            send_sem=pay_send.at[k],
            recv_sem=pay_recv.at[k],
            device_id=(peer, s),
            device_id_type=MESH,
        )

    def rec_copy(k):
        peer = lax.rem(g + k, nb)
        return pltpu.make_async_remote_copy(
            src_ref=records.at[peer],
            dst_ref=rec_same.at[g],
            send_sem=rec_send.at[k],
            recv_sem=rec_recv.at[k],
            device_id=(peer, s),
            device_id_type=MESH,
        )

    def left_copy(k):
        peer = lax.rem(g + k, nb)
        return pltpu.make_async_remote_copy(
            src_ref=records.at[peer],
            dst_ref=rec_left.at[g],
            send_sem=left_send.at[k],
            recv_sem=left_recv.at[k],
            device_id=(peer, right),
            device_id_type=MESH,
        )

    def start_far(k, carry):
        rec_copy(k).start()
        left_copy(k).start()
        pay_copy(k).start()
        return carry

    left_copy(0).start()
    lax.fori_loop(1, nb, start_far, 0)
    own = [
        pltpu.make_async_copy(packed.at[mine], moved_hbm.at[mine], own_sem.at[0]),
        pltpu.make_async_copy(records.at[g], rec_same.at[g], own_sem.at[1]),
    ]
    for copy in own:
        copy.start()

    for copy in halo[2:4]:
        copy.wait()

    def first(i, carry):
        row = pl.multiple_of(i * 8, 8)
        here, term = step_term(
            f0, row + DEEP - THIN, flow[0, pl.ds(row, 8), :], flow[1, pl.ds(row, 8), :]
        )
        f1[pl.ds(row + DEEP - THIN, 8), :] = here + STEP * term
        return carry

    def first_inner(i, carry):
        row = pl.multiple_of(i * 8, 8)
        rows = pl.ds(row + DEEP - THIN, 8)
        here = f0[rows, :]
        along_x = column_term(here, flow[0, pl.ds(row, 8), :])
        end_y = row_term(f0, row + DEEP - THIN, end, flow[1, pl.ds(row, 8), end])
        along_y = jnp.concatenate([f1[rows, wide], end_y], axis=1)
        f1[rows, :] = here - STEP * (along_x + along_y)
        return carry

    chunks = (height + 2 * THIN) // 8
    lax.fori_loop(0, 2, first, 0)
    lax.fori_loop(2, chunks - 2, first_inner, 0)
    lax.fori_loop(chunks - 2, chunks, first, 0)

    def second(i, carry):
        row = pl.multiple_of(i * 8, 8)
        here, term = step_term(
            f1, row + DEEP - THIN, flow[0, pl.ds(row, 8), :], flow[1, pl.ds(row, 8), :]
        )
        at = pl.ds(row + DEEP - THIN, 8)
        f2[at, :] = 0.75 * f0[at, :] + 0.25 * (here + STEP * term)
        return carry

    lax.fori_loop(0, (height + 2 * THIN) // 8, second, 0)

    def third(i, carry):
        row = pl.multiple_of(i * 8, 8)
        at = pl.ds(row + THIN, 8)
        here, term = step_term(f2, row + DEEP, flow[0, at, :], flow[1, at, :])
        value = f0[pl.ds(row + DEEP, 8), :] / 3.0 + 2.0 / 3.0 * (here + STEP * term)
        out_ref[pl.ds(row, 8), :] = value[:, :across]
        return carry

    lax.fori_loop(0, height // 8, third, 0)

    for copy in own:
        copy.wait()
    left_copy(0).wait()

    def finish_far(k, carry):
        rec_copy(k).wait()
        left_copy(k).wait()
        return carry

    lax.fori_loop(1, nb, finish_far, 0)

    row_lane = lax.broadcasted_iota(jnp.int32, (nb, LANES), 1).astype(jnp.float32)
    lane_out = lax.broadcasted_iota(jnp.int32, (nb, across), 1).astype(jnp.float32)
    spread = 2 * CAP

    def slots_of(box):
        for j in range(spread):
            fields = [box[:, k * spread + j : k * spread + j + 1] for k in range(6)]
            if j >= CAP:
                fields[0] = fields[0] - float(height)
            yield fields

    def laid(hots, rows):
        hot = jnp.transpose(jnp.concatenate(hots, axis=0))[:height]
        return chosen(hot, jnp.concatenate(rows, axis=0))

    hots, rows = [], []
    for row, col, low_low, high_low, low_high, high_high in slots_of(
        jnp.concatenate([rec_same[k] for k in range(nb)], axis=0)
    ):
        here, beside = lane_out == col, lane_out == col + 1.0
        hots += [(row_lane == row).astype(jnp.float32), (row_lane == row + 1.0).astype(jnp.float32)]
        rows += [
            jnp.where(here, low_low, jnp.where(beside, low_high, 0.0)),
            jnp.where(here, high_low, jnp.where(beside, high_high, 0.0)),
        ]
    out_ref[...] += laid(hots, rows)
    hots, rows = [], []
    for row, col, low_low, high_low, low_high, high_high in slots_of(
        jnp.concatenate([rec_left[k] for k in range(nb)], axis=0)
    ):
        spill = (col == float(across - 1)) & (row_lane == 0.0)
        hots += [(row_lane == row).astype(jnp.float32), (row_lane == row + 1.0).astype(jnp.float32)]
        rows += [jnp.where(spill, low_high, 0.0), jnp.where(spill, high_high, 0.0)]
    out_ref[:, 0:LANES] += laid(hots, rows)

    def finish_pay(k, carry):
        pay_copy(k).wait()
        return carry

    lax.fori_loop(1, nb, finish_pay, 0)


def shards(nb, nx, level_set, velocity, particles, escaped, home, land, dest, count):
    height, across = level_set.shape
    total, kinds, per_block = particles.shape
    width = across + LANES
    rows = nb * CAP * FIELDS
    halos = 10 if nx > 2 else 7
    vmem = pl.BlockSpec(memory_space=pltpu.VMEM)
    f32 = jnp.float32
    dma = pltpu.SemaphoreType.DMA
    level, moved = pl.pallas_call(
        functools.partial(kernel, nb, nx),
        out_shape=(
            pltpu.VMEM((height, across), f32),
            pltpu.VMEM((rows, per_block), f32),
        ),
        in_specs=[pl.BlockSpec(memory_space=pltpu.HBM)] * 8,
        out_specs=(vmem, vmem),
        scratch_shapes=[
            pltpu.VMEM((height + 2 * DEEP, width), f32),
            pltpu.VMEM((2, height + 2 * THIN, width), f32),
            pltpu.VMEM((height + 2 * DEEP, width), f32),
            pltpu.VMEM((height + 2 * DEEP, width), f32),
            pltpu.VMEM((height, LANES), f32),
            pltpu.VMEM((height + 2 * DEEP, LANES), f32),
            pltpu.VMEM((height + 2 * DEEP, LANES), f32),
            pltpu.VMEM((kinds, total, per_block), f32),
            pltpu.VMEM(escaped.shape, jnp.int32),
            pltpu.VMEM(home.shape, jnp.int32),
            pltpu.VMEM(land.shape, jnp.int32),
            pltpu.VMEM(dest.shape, jnp.int32),
            pltpu.SMEM(count.shape, jnp.int32),
            pltpu.VMEM((rows, per_block), f32),
            pltpu.VMEM((nb, 1, LANES), f32),
            pltpu.VMEM((nb, 1, LANES), f32),
            pltpu.VMEM((nb, 1, LANES), f32),
            dma((8,)),
            dma((halos,)),
            dma((halos,)),
            dma((nb,)),
            dma((nb,)),
            dma((nb,)),
            dma((nb,)),
            dma((nb,)),
            dma((nb,)),
            dma((2,)),
        ],
        compiler_params=pltpu.CompilerParams(collective_id=0, has_side_effects=True),
    )(
        level_set,
        velocity,
        jnp.transpose(particles, (1, 0, 2)),
        escaped,
        home,
        land,
        dest,
        count,
    )
    return level, moved.reshape(nb * CAP, FIELDS, per_block)


def solution(mesh):
    in_specs = (
        P("gy", "gx"),
        P(None, "gy", "gx"),
        P(("gy", "gx"), None, None),
        P(("gy", "gx"), None),
        P(("gy", "gx")),
        P(("gy", "gx")),
        P(("gy", "gx")),
        P(("gy", "gx")),
    )
    out_specs = (P("gy", "gx"), P(("gy", "gx"), None, None))
    body = functools.partial(shards, mesh.shape["gy"], mesh.shape["gx"])
    return jax.shard_map(body, mesh=mesh, in_specs=in_specs, out_specs=out_specs, check_vma=False)
```

```python
import functools

import jax
import jax.numpy as jnp
from jax import lax
from jax.experimental import pallas as pl
from jax.experimental.pallas import tpu as pltpu
from jax.sharding import PartitionSpec as P

CAP = 4
FIELDS = 4
STEP = 0.3
EPS4 = 4e-06
LANES = 128
DEEP = 16
THIN = 8
MESH = pl.DeviceIdType.MESH


def one_sided(speed, lower, upper, s_m2, s_m1, s_0, s_p1, s_p2):
    ahead = speed > 0
    c = jnp.where(ahead, lower, upper)
    p = jnp.where(ahead, s_m2, s_p2)
    q = jnp.where(ahead, s_m1, s_p1)
    r = s_0
    w = jnp.where(ahead, s_p1, s_m1)
    k = 13.0 / 3.0
    a1, b1 = p - q, p - 3.0 * q
    a2, b2 = q - r, q + r
    a3, b3 = r - w, 3.0 * r - w
    t1 = k * (a1 * a1) + (b1 * b1 + EPS4)
    t2 = k * (a2 * a2) + (b2 * b2 + EPS4)
    t3 = k * (a3 * a3) + (b3 * b3 + EPS4)
    m1, m2, m3 = t2 * t3, t1 * t3, t1 * t2
    w1 = m1 * m1
    w2 = 6.0 * (m2 * m2)
    w3 = 3.0 * (m3 * m3)
    top = w1 * (2.0 * p - 5.0 * q) - w2 * (q + 2.0 * r) + w3 * (w - 4.0 * r)
    bottom = w1 + w2 + w3
    return speed * c - (jnp.abs(speed) * (1.0 / 6.0)) * (top / bottom)


def row_term(field, row, lanes, v):
    window = field[pl.ds(pl.multiple_of(row - 8, 8), 24), lanes]
    taps = [pltpu.roll(window, (24 - k) % 24, 0)[8:16] for k in range(-3, 4)]
    d = [taps[k + 1] - taps[k] for k in range(6)]
    s = [d[k + 1] - d[k] for k in range(5)]
    return one_sided(v, d[2], d[3], *s)


def column_term(here, u):
    width = here.shape[1]
    upper = pltpu.roll(here, width - 1, 1) - here
    lower = here - pltpu.roll(here, 1, 1)
    mid = upper - lower
    return one_sided(
        u,
        lower,
        upper,
        pltpu.roll(mid, 2, 1),
        pltpu.roll(mid, 1, 1),
        mid,
        pltpu.roll(mid, width - 1, 1),
        pltpu.roll(mid, width - 2, 1),
    )


def step_term(field, row, u, v):
    here = field[pl.ds(pl.multiple_of(row, 8), 8), :]
    return here, -(column_term(here, u) + row_term(field, row, slice(None), v))


def pieces(x):
    top = x.astype(jnp.bfloat16)
    rest = x - top.astype(jnp.float32)
    middle = rest.astype(jnp.bfloat16)
    return top, middle, (rest - middle.astype(jnp.float32)).astype(jnp.bfloat16)


def chosen(hot, x):
    hot = hot.astype(jnp.bfloat16)
    top, middle, last = (
        jnp.dot(hot, part, preferred_element_type=jnp.float32) for part in pieces(x)
    )
    return top + (middle + last)


def kernel(
    nb,
    nx,
    level_hbm,
    flow_hbm,
    parts_hbm,
    escaped_hbm,
    home_hbm,
    land_hbm,
    dest_hbm,
    count_hbm,
    out_ref,
    moved_hbm,
    f0,
    flow,
    f1,
    f2,
    side,
    from_left,
    from_right,
    parts,
    escaped,
    home_ref,
    land_ref,
    dest_ref,
    count_ref,
    packed,
    records,
    rec_same,
    rec_left,
    load_sem,
    halo_send,
    halo_recv,
    pay_send,
    pay_recv,
    rec_send,
    rec_recv,
    left_send,
    left_recv,
    own_sem,
):
    g = lax.axis_index("gy")
    s = lax.axis_index("gx")
    height, across = level_hbm.shape
    width = across + LANES
    total = parts_hbm.shape[1]
    up = lax.rem(g + nb - 1, nb)
    down = lax.rem(g + 1, nb)
    left = lax.rem(s + nx - 1, nx)
    right = lax.rem(s + 1, nx)

    barrier = pltpu.get_barrier_semaphore()
    offsets = sorted({0, 1 % nx, (nx - 1) % nx})
    for off in offsets:
        strip = lax.rem(s + off, nx)

        def greet(k, carry, strip=strip):
            pl.semaphore_signal(
                barrier, inc=1, device_id=(lax.rem(g + k, nb), strip), device_id_type=MESH
            )
            return carry

        lax.fori_loop(1 if off == 0 else 0, nb, greet, 0)

    loads = [
        pltpu.make_async_copy(
            level_hbm, f0.at[pl.ds(DEEP, height), pl.ds(0, across)], load_sem.at[0]
        ),
        pltpu.make_async_copy(
            flow_hbm, flow.at[:, pl.ds(THIN, height), pl.ds(0, across)], load_sem.at[1]
        ),
        pltpu.make_async_copy(parts_hbm, parts, load_sem.at[2]),
        pltpu.make_async_copy(escaped_hbm, escaped, load_sem.at[3]),
    ]
    small = [
        pltpu.make_async_copy(src, dst, load_sem.at[4 + k])
        for k, (src, dst) in enumerate(
            (
                (home_hbm, home_ref),
                (land_hbm, land_ref),
                (dest_hbm, dest_ref),
                (count_hbm, count_ref),
            )
        )
    ]
    for copy in small + loads:
        copy.start()
    for copy in small:
        copy.wait()

    home = home_ref[...].reshape(1, total)
    land = land_ref[...].reshape(1, total)
    dest = dest_ref[...].reshape(1, total)
    lane = lax.broadcasted_iota(jnp.int32, (total, total), 1)
    sub = lax.broadcasted_iota(jnp.int32, (total, total), 0)

    def upright(row):
        return jnp.sum(jnp.where(lane == sub, row, 0), axis=1, keepdims=True)

    dest_col = upright(dest)
    home_col = upright(home)
    land_col = upright(land)
    live = count_ref[0]
    earlier = (dest == dest_col) & (sub < lane) & (sub < live)
    rank = jnp.sum(earlier.astype(jnp.int32), axis=0, keepdims=True)
    is_live = lax.broadcasted_iota(jnp.int32, (1, total), 1) < live
    slot = jnp.where(is_live, dest * CAP + rank, -1)
    rank_col = upright(rank)
    own_band = jnp.where(is_live, dest, -1)
    past_band = jnp.where(is_live, jnp.where(dest == nb - 1, 0, dest + 1), -1)

    pl.semaphore_wait(barrier, nb * len(offsets) - 1)

    halo = []

    def send(src, dst, band, strip):
        i = len(halo)
        copy = pltpu.make_async_remote_copy(
            src_ref=src,
            dst_ref=dst,
            send_sem=halo_send.at[i],
            recv_sem=halo_recv.at[i],
            device_id=(band, strip),
            device_id_type=MESH,
        )
        copy.start()
        halo.append(copy)

    wide = pl.ds(0, across)
    send(
        flow_hbm.at[:, pl.ds(0, THIN)], flow.at[:, pl.ds(THIN + height, THIN), wide], up, s
    )
    send(
        flow_hbm.at[:, pl.ds(height - THIN, THIN)], flow.at[:, pl.ds(0, THIN), wide], down, s
    )
    send(level_hbm.at[pl.ds(0, DEEP)], f0.at[pl.ds(DEEP + height, DEEP), wide], up, s)
    send(level_hbm.at[pl.ds(height - DEEP, DEEP)], f0.at[pl.ds(0, DEEP), wide], down, s)

    loads[0].wait()
    loads[1].wait()

    spot = lax.broadcasted_iota(jnp.int32, (height, LANES), 1)
    low = [
        f0[pl.ds(DEEP, height), 0:LANES],
        pltpu.roll(flow[0, pl.ds(THIN, height), 0:LANES], 16, 1),
        pltpu.roll(flow[1, pl.ds(THIN, height), 0:LANES], 32, 1),
    ]
    tail = pl.ds(across - LANES, LANES)
    high = [
        f0[pl.ds(DEEP, height), tail],
        pltpu.roll(flow[0, pl.ds(THIN, height), tail], LANES - 16, 1),
        pltpu.roll(flow[1, pl.ds(THIN, height), tail], LANES - 32, 1),
    ]
    low_edge = jnp.where(spot < 16, low[0], jnp.where(spot < 32, low[1], low[2]))
    high_edge = jnp.where(spot >= 112, high[0], jnp.where(spot >= 96, high[1], high[2]))
    side[...] = jnp.where(spot < 64, low_edge, high_edge)

    for box, strip in ((from_right, left), (from_left, right))[: 2 if nx > 2 else 1]:
        send(side, box.at[pl.ds(DEEP, height)], g, strip)
        send(side.at[pl.ds(0, DEEP)], box.at[pl.ds(DEEP + height, DEEP)], up, strip)
        send(side.at[pl.ds(height - DEEP, DEEP)], box.at[pl.ds(0, DEEP)], down, strip)
    loads[2].wait()
    loads[3].wait()
    radius = parts[2]
    weight = escaped[...].astype(jnp.float32) * radius

    home_row = home_col // across
    home_at = home_col - home_row * across
    pick_lane = lax.broadcasted_iota(jnp.int32, (total, THIN + height), 1)
    pick = jnp.concatenate(
        [
            (pick_lane == home_row).astype(jnp.float32),
            (pick_lane == home_row + 1).astype(jnp.float32),
        ],
        axis=0,
    )
    slot_row = lax.broadcasted_iota(jnp.int32, (nb * CAP, total), 0)
    slot_hot = (slot_row == slot).astype(jnp.float32)
    band_row = lax.broadcasted_iota(jnp.int32, (nb, total), 0)
    own_hot = (band_row == own_band).astype(jnp.float32)
    past_hot = (band_row == past_band).astype(jnp.float32)
    land_row = land_col // across

    column = lax.broadcasted_iota(jnp.int32, (total, across), 1)
    this_column = column == home_at
    next_column = column == home_at + 1
    at_last = home_row == height - 1
    at_edge = home_at == across - 1
    fraction_y = parts[1] + 0.5
    fraction_x = parts[0] + 0.5

    def at(rows, mask):
        return jnp.sum(jnp.where(mask, rows, 0.0), axis=1, keepdims=True)

    inside = []
    for component in range(2):
        both = chosen(pick[:, :height], flow[component, pl.ds(THIN, height), wide])
        inside.append(
            [
                at(both[low : low + total], mask)
                for mask in (this_column, next_column)
                for low in (0, total)
            ]
        )

    def early(i, carry):
        row = pl.multiple_of(i * 8, 8)
        rows = pl.ds(row + DEEP - THIN, 8)
        f1[rows, wide] = row_term(f0, row + DEEP - THIN, wide, flow[1, pl.ds(row, 8), wide])
        return carry

    lax.fori_loop(2, height // 8, early, 0)

    for copy in halo[:2] + halo[4:]:
        copy.wait()

    spot = lax.broadcasted_iota(jnp.int32, (height + 2 * DEEP, LANES), 1)
    after = from_right[...]
    before = from_left[...] if nx > 2 else after
    end = pl.ds(across, LANES)
    f0[:, end] = jnp.where(spot < 64, after, before)
    inner = slice(DEEP - THIN, DEEP + height + THIN)
    spot, after, before = spot[inner], after[inner], before[inner]
    flow[0, :, end] = jnp.where(
        spot < 64, pltpu.roll(after, LANES - 16, 1), pltpu.roll(before, 16, 1)
    )
    flow[1, :, end] = jnp.where(
        spot < 64, pltpu.roll(after, LANES - 32, 1), pltpu.roll(before, 32, 1)
    )

    def mixture(component):
        low_low, high_low, low_high, high_high = inside[component]
        below = flow[component, pl.ds(THIN + height, THIN), wide][0:1]
        beyond = chosen(pick, flow[component, pl.ds(THIN, height + THIN), end])[:, 0:1]
        high_low = high_low + jnp.where(at_last, at(below, this_column), 0.0)
        high_high = high_high + jnp.where(at_last, at(below, next_column), 0.0)
        low_high = low_high + jnp.where(at_edge, beyond[:total], 0.0)
        high_high = high_high + jnp.where(at_edge, beyond[total:], 0.0)
        return (
            (1.0 - fraction_y) * (1.0 - fraction_x) * low_low
            + fraction_y * (1.0 - fraction_x) * high_low
            + (1.0 - fraction_y) * fraction_x * low_high
            + fraction_y * fraction_x * high_high
        )

    new_x = parts[0] + STEP * mixture(0)
    new_y = parts[1] + STEP * mixture(1)

    payload = chosen(slot_hot, jnp.concatenate([new_x, new_y, radius, weight], axis=1))
    for k in range(FIELDS):
        packed[pl.ds(k, nb * CAP, stride=FIELDS), :] = payload[:, k * LANES : (k + 1) * LANES]

    gy = new_y + 0.5
    gx = new_x + 0.5

    def over(rows):
        return jnp.sum(rows, axis=1, keepdims=True)

    columns = (
        land_row.astype(jnp.float32),
        (land_col - land_row * across).astype(jnp.float32),
        over(weight * (1.0 - gy) * (1.0 - gx)),
        over(weight * gy * (1.0 - gx)),
        over(weight * (1.0 - gy) * gx),
        over(weight * gy * gx),
    )
    spot = lax.broadcasted_iota(jnp.int32, (total, LANES), 1)
    table = jnp.zeros((total, LANES), jnp.float32)
    for k, one in enumerate(columns):
        table = jnp.where(spot // (2 * CAP) == k, one, table)
    place = spot % (2 * CAP)
    sheet = chosen(own_hot, jnp.where(place == rank_col, table, 0.0)) + chosen(
        past_hot, jnp.where(place == rank_col + CAP, table, 0.0)
    )
    for band in range(nb):
        records[band] = sheet[band : band + 1]

    per = CAP * FIELDS
    mine = pl.ds(pl.multiple_of(g * per, per), per)

    def pay_copy(k):
        peer = lax.rem(g + k, nb)
        return pltpu.make_async_remote_copy(
            src_ref=packed.at[pl.ds(pl.multiple_of(peer * per, per), per)],
            dst_ref=moved_hbm.at[mine],
            send_sem=pay_send.at[k],
            recv_sem=pay_recv.at[k],
            device_id=(peer, s),
            device_id_type=MESH,
        )

    def rec_copy(k):
        peer = lax.rem(g + k, nb)
        return pltpu.make_async_remote_copy(
            src_ref=records.at[peer],
            dst_ref=rec_same.at[g],
            send_sem=rec_send.at[k],
            recv_sem=rec_recv.at[k],
            device_id=(peer, s),
            device_id_type=MESH,
        )

    def left_copy(k):
        peer = lax.rem(g + k, nb)
        return pltpu.make_async_remote_copy(
            src_ref=records.at[peer],
            dst_ref=rec_left.at[g],
            send_sem=left_send.at[k],
            recv_sem=left_recv.at[k],
            device_id=(peer, right),
            device_id_type=MESH,
        )

    def start_far(k, carry):
        rec_copy(k).start()
        left_copy(k).start()
        pay_copy(k).start()
        return carry

    left_copy(0).start()
    lax.fori_loop(1, nb, start_far, 0)
    own = [
        pltpu.make_async_copy(packed.at[mine], moved_hbm.at[mine], own_sem.at[0]),
        pltpu.make_async_copy(records.at[g], rec_same.at[g], own_sem.at[1]),
    ]
    for copy in own:
        copy.start()

    for copy in halo[2:4]:
        copy.wait()

    def first(i, carry):
        row = pl.multiple_of(i * 8, 8)
        here, term = step_term(
            f0, row + DEEP - THIN, flow[0, pl.ds(row, 8), :], flow[1, pl.ds(row, 8), :]
        )
        f1[pl.ds(row + DEEP - THIN, 8), :] = here + STEP * term
        return carry

    def first_inner(i, carry):
        row = pl.multiple_of(i * 8, 8)
        rows = pl.ds(row + DEEP - THIN, 8)
        here = f0[rows, :]
        along_x = column_term(here, flow[0, pl.ds(row, 8), :])
        end_y = row_term(f0, row + DEEP - THIN, end, flow[1, pl.ds(row, 8), end])
        along_y = jnp.concatenate([f1[rows, wide], end_y], axis=1)
        f1[rows, :] = here - STEP * (along_x + along_y)
        return carry

    chunks = (height + 2 * THIN) // 8
    lax.fori_loop(0, 2, first, 0)
    lax.fori_loop(2, chunks - 2, first_inner, 0)
    lax.fori_loop(chunks - 2, chunks, first, 0)

    def second(i, carry):
        row = pl.multiple_of(i * 8, 8)
        here, term = step_term(
            f1, row + DEEP - THIN, flow[0, pl.ds(row, 8), :], flow[1, pl.ds(row, 8), :]
        )
        at = pl.ds(row + DEEP - THIN, 8)
        f2[at, :] = 0.75 * f0[at, :] + 0.25 * (here + STEP * term)
        return carry

    lax.fori_loop(0, (height + 2 * THIN) // 8, second, 0)

    def third(i, carry):
        row = pl.multiple_of(i * 8, 8)
        at = pl.ds(row + THIN, 8)
        here, term = step_term(f2, row + DEEP, flow[0, at, :], flow[1, at, :])
        value = f0[pl.ds(row + DEEP, 8), :] / 3.0 + 2.0 / 3.0 * (here + STEP * term)
        out_ref[pl.ds(row, 8), :] = value[:, :across]
        return carry

    lax.fori_loop(0, height // 8, third, 0)

    for copy in own:
        copy.wait()
    left_copy(0).wait()

    def finish_far(k, carry):
        rec_copy(k).wait()
        left_copy(k).wait()
        return carry

    lax.fori_loop(1, nb, finish_far, 0)

    row_lane = lax.broadcasted_iota(jnp.int32, (nb, LANES), 1).astype(jnp.float32)
    lane_out = lax.broadcasted_iota(jnp.int32, (nb, across), 1).astype(jnp.float32)
    spread = 2 * CAP

    def slots_of(box):
        for j in range(spread):
            fields = [box[:, k * spread + j : k * spread + j + 1] for k in range(6)]
            if j >= CAP:
                fields[0] = fields[0] - float(height)
            yield fields

    def laid(hots, rows):
        hot = jnp.transpose(jnp.concatenate(hots, axis=0))[:height]
        return chosen(hot, jnp.concatenate(rows, axis=0))

    hots, rows = [], []
    for row, col, low_low, high_low, low_high, high_high in slots_of(
        jnp.concatenate([rec_same[k] for k in range(nb)], axis=0)
    ):
        here, beside = lane_out == col, lane_out == col + 1.0
        hots += [(row_lane == row).astype(jnp.float32), (row_lane == row + 1.0).astype(jnp.float32)]
        rows += [
            jnp.where(here, low_low, jnp.where(beside, low_high, 0.0)),
            jnp.where(here, high_low, jnp.where(beside, high_high, 0.0)),
        ]
    out_ref[...] += laid(hots, rows)
    hots, rows = [], []
    for row, col, low_low, high_low, low_high, high_high in slots_of(
        jnp.concatenate([rec_left[k] for k in range(nb)], axis=0)
    ):
        spill = (col == float(across - 1)) & (row_lane == 0.0)
        hots += [(row_lane == row).astype(jnp.float32), (row_lane == row + 1.0).astype(jnp.float32)]
        rows += [jnp.where(spill, low_high, 0.0), jnp.where(spill, high_high, 0.0)]
    out_ref[:, 0:LANES] += laid(hots, rows)

    def finish_pay(k, carry):
        pay_copy(k).wait()
        return carry

    lax.fori_loop(1, nb, finish_pay, 0)


def settle(level_ref, moved_ref, level_hbm, moved_hbm, sem):
    copies = [
        pltpu.make_async_copy(level_ref, level_hbm, sem.at[0]),
        pltpu.make_async_copy(moved_ref, moved_hbm, sem.at[1]),
    ]
    for copy in copies:
        copy.start()
    for copy in copies:
        copy.wait()


def shards(nb, nx, level_set, velocity, particles, escaped, home, land, dest, count):
    height, across = level_set.shape
    total, kinds, per_block = particles.shape
    width = across + LANES
    rows = nb * CAP * FIELDS
    halos = 10 if nx > 2 else 7
    vmem = pl.BlockSpec(memory_space=pltpu.VMEM)
    f32 = jnp.float32
    dma = pltpu.SemaphoreType.DMA
    level, moved = pl.pallas_call(
        functools.partial(kernel, nb, nx),
        out_shape=(
            pltpu.VMEM((height, across), f32),
            pltpu.VMEM((rows, per_block), f32),
        ),
        in_specs=[pl.BlockSpec(memory_space=pltpu.HBM)] * 8,
        out_specs=(vmem, vmem),
        scratch_shapes=[
            pltpu.VMEM((height + 2 * DEEP, width), f32),
            pltpu.VMEM((2, height + 2 * THIN, width), f32),
            pltpu.VMEM((height + 2 * DEEP, width), f32),
            pltpu.VMEM((height + 2 * DEEP, width), f32),
            pltpu.VMEM((height, LANES), f32),
            pltpu.VMEM((height + 2 * DEEP, LANES), f32),
            pltpu.VMEM((height + 2 * DEEP, LANES), f32),
            pltpu.VMEM((kinds, total, per_block), f32),
            pltpu.VMEM(escaped.shape, jnp.int32),
            pltpu.VMEM(home.shape, jnp.int32),
            pltpu.VMEM(land.shape, jnp.int32),
            pltpu.VMEM(dest.shape, jnp.int32),
            pltpu.SMEM(count.shape, jnp.int32),
            pltpu.VMEM((rows, per_block), f32),
            pltpu.VMEM((nb, 1, LANES), f32),
            pltpu.VMEM((nb, 1, LANES), f32),
            pltpu.VMEM((nb, 1, LANES), f32),
            dma((8,)),
            dma((halos,)),
            dma((halos,)),
            dma((nb,)),
            dma((nb,)),
            dma((nb,)),
            dma((nb,)),
            dma((nb,)),
            dma((nb,)),
            dma((2,)),
        ],
        compiler_params=pltpu.CompilerParams(collective_id=0, has_side_effects=True),
    )(
        level_set,
        velocity,
        jnp.transpose(particles, (1, 0, 2)),
        escaped,
        home,
        land,
        dest,
        count,
    )
    level, moved = pl.pallas_call(
        settle,
        out_shape=(
            jax.ShapeDtypeStruct((height, across), f32),
            jax.ShapeDtypeStruct((rows, per_block), f32),
        ),
        in_specs=[vmem, vmem],
        out_specs=(pl.BlockSpec(memory_space=pl.ANY),) * 2,
        scratch_shapes=[dma((2,))],
    )(
        pltpu.with_memory_space_constraint(level, pltpu.VMEM),
        pltpu.with_memory_space_constraint(moved, pltpu.VMEM),
    )
    return level, moved.reshape(nb * CAP, FIELDS, per_block)


def solution(mesh):
    in_specs = (
        P("gy", "gx"),
        P(None, "gy", "gx"),
        P(("gy", "gx"), None, None),
        P(("gy", "gx"), None),
        P(("gy", "gx")),
        P(("gy", "gx")),
        P(("gy", "gx")),
        P(("gy", "gx")),
    )
    out_specs = (P("gy", "gx"), P(("gy", "gx"), None, None))
    body = functools.partial(shards, mesh.shape["gy"], mesh.shape["gx"])
    return jax.shard_map(body, mesh=mesh, in_specs=in_specs, out_specs=out_specs, check_vma=False)
```

```python
import functools

import jax
import jax.numpy as jnp
from jax import lax
from jax.experimental import pallas as pl
from jax.experimental.pallas import tpu as pltpu
from jax.sharding import PartitionSpec as P

CAP = 4
FIELDS = 4
STEP = 0.3
EPS4 = 4e-06
LANES = 128
DEEP = 16
THIN = 8
MESH = pl.DeviceIdType.MESH


def one_sided(speed, lower, upper, s_m2, s_m1, s_0, s_p1, s_p2):
    ahead = speed > 0
    c = jnp.where(ahead, lower, upper)
    p = jnp.where(ahead, s_m2, s_p2)
    q = jnp.where(ahead, s_m1, s_p1)
    r = s_0
    w = jnp.where(ahead, s_p1, s_m1)
    k = 13.0 / 3.0
    a1, b1 = p - q, p - 3.0 * q
    a2, b2 = q - r, q + r
    a3, b3 = r - w, 3.0 * r - w
    t1 = k * (a1 * a1) + (b1 * b1 + EPS4)
    t2 = k * (a2 * a2) + (b2 * b2 + EPS4)
    t3 = k * (a3 * a3) + (b3 * b3 + EPS4)
    m1, m2, m3 = t2 * t3, t1 * t3, t1 * t2
    w1 = m1 * m1
    w2 = 6.0 * (m2 * m2)
    w3 = 3.0 * (m3 * m3)
    top = w1 * (2.0 * p - 5.0 * q) - w2 * (q + 2.0 * r) + w3 * (w - 4.0 * r)
    bottom = w1 + w2 + w3
    return speed * c - (jnp.abs(speed) * (1.0 / 6.0)) * (top / bottom)


def row_term(field, row, lanes, v):
    window = field[pl.ds(pl.multiple_of(row - 8, 8), 24), lanes]
    taps = [pltpu.roll(window, (24 - k) % 24, 0)[8:16] for k in range(-3, 4)]
    d = [taps[k + 1] - taps[k] for k in range(6)]
    s = [d[k + 1] - d[k] for k in range(5)]
    return one_sided(v, d[2], d[3], *s)


def column_term(here, u):
    width = here.shape[1]
    upper = pltpu.roll(here, width - 1, 1) - here
    lower = here - pltpu.roll(here, 1, 1)
    mid = upper - lower
    return one_sided(
        u,
        lower,
        upper,
        pltpu.roll(mid, 2, 1),
        pltpu.roll(mid, 1, 1),
        mid,
        pltpu.roll(mid, width - 1, 1),
        pltpu.roll(mid, width - 2, 1),
    )


def step_term(field, row, u, v):
    here = field[pl.ds(pl.multiple_of(row, 8), 8), :]
    return here, -(column_term(here, u) + row_term(field, row, slice(None), v))


def pieces(x):
    top = x.astype(jnp.bfloat16)
    rest = x - top.astype(jnp.float32)
    middle = rest.astype(jnp.bfloat16)
    return top, middle, (rest - middle.astype(jnp.float32)).astype(jnp.bfloat16)


def chosen(hot, x):
    hot = hot.astype(jnp.bfloat16)
    top, middle, last = (
        jnp.dot(hot, part, preferred_element_type=jnp.float32) for part in pieces(x)
    )
    return top + (middle + last)


def kernel(
    nb,
    nx,
    level_hbm,
    flow_hbm,
    parts_hbm,
    escaped_hbm,
    home_hbm,
    land_hbm,
    dest_hbm,
    count_hbm,
    out_ref,
    moved_hbm,
    f0,
    flow,
    f1,
    f2,
    side,
    from_left,
    from_right,
    parts,
    escaped,
    home_ref,
    land_ref,
    dest_ref,
    count_ref,
    packed,
    records,
    rec_same,
    rec_left,
    load_sem,
    halo_send,
    halo_recv,
    pay_send,
    pay_recv,
    rec_send,
    rec_recv,
    left_send,
    left_recv,
    own_sem,
):
    g = lax.axis_index("gy")
    s = lax.axis_index("gx")
    height, across = level_hbm.shape
    width = across + LANES
    total = parts_hbm.shape[1]
    up = lax.rem(g + nb - 1, nb)
    down = lax.rem(g + 1, nb)
    left = lax.rem(s + nx - 1, nx)
    right = lax.rem(s + 1, nx)

    barrier = pltpu.get_barrier_semaphore()
    offsets = sorted({0, 1 % nx, (nx - 1) % nx})
    for off in offsets:
        strip = lax.rem(s + off, nx)

        def greet(k, carry, strip=strip):
            pl.semaphore_signal(
                barrier, inc=1, device_id=(lax.rem(g + k, nb), strip), device_id_type=MESH
            )
            return carry

        lax.fori_loop(1 if off == 0 else 0, nb, greet, 0)

    loads = [
        pltpu.make_async_copy(
            level_hbm, f0.at[pl.ds(DEEP, height), pl.ds(0, across)], load_sem.at[0]
        ),
        pltpu.make_async_copy(
            flow_hbm, flow.at[:, pl.ds(THIN, height), pl.ds(0, across)], load_sem.at[1]
        ),
        pltpu.make_async_copy(parts_hbm, parts, load_sem.at[2]),
        pltpu.make_async_copy(escaped_hbm, escaped, load_sem.at[3]),
    ]
    small = [
        pltpu.make_async_copy(src, dst, load_sem.at[4 + k])
        for k, (src, dst) in enumerate(
            (
                (home_hbm, home_ref),
                (land_hbm, land_ref),
                (dest_hbm, dest_ref),
                (count_hbm, count_ref),
            )
        )
    ]
    for copy in small + loads:
        copy.start()
    for copy in small:
        copy.wait()

    home = home_ref[...].reshape(1, total)
    land = land_ref[...].reshape(1, total)
    dest = dest_ref[...].reshape(1, total)
    lane = lax.broadcasted_iota(jnp.int32, (total, total), 1)
    sub = lax.broadcasted_iota(jnp.int32, (total, total), 0)

    def upright(row):
        return jnp.sum(jnp.where(lane == sub, row, 0), axis=1, keepdims=True)

    dest_col = upright(dest)
    home_col = upright(home)
    land_col = upright(land)
    live = count_ref[0]
    earlier = (dest == dest_col) & (sub < lane) & (sub < live)
    rank = jnp.sum(earlier.astype(jnp.int32), axis=0, keepdims=True)
    is_live = lax.broadcasted_iota(jnp.int32, (1, total), 1) < live
    slot = jnp.where(is_live, dest * CAP + rank, -1)
    rank_col = upright(rank)
    own_band = jnp.where(is_live, dest, -1)
    past_band = jnp.where(is_live, jnp.where(dest == nb - 1, 0, dest + 1), -1)

    pl.semaphore_wait(barrier, nb * len(offsets) - 1)

    halo = []

    def send(src, dst, band, strip):
        i = len(halo)
        copy = pltpu.make_async_remote_copy(
            src_ref=src,
            dst_ref=dst,
            send_sem=halo_send.at[i],
            recv_sem=halo_recv.at[i],
            device_id=(band, strip),
            device_id_type=MESH,
        )
        copy.start()
        halo.append(copy)

    wide = pl.ds(0, across)
    send(
        flow_hbm.at[:, pl.ds(0, THIN)], flow.at[:, pl.ds(THIN + height, THIN), wide], up, s
    )
    send(
        flow_hbm.at[:, pl.ds(height - THIN, THIN)], flow.at[:, pl.ds(0, THIN), wide], down, s
    )
    send(level_hbm.at[pl.ds(0, DEEP)], f0.at[pl.ds(DEEP + height, DEEP), wide], up, s)
    send(level_hbm.at[pl.ds(height - DEEP, DEEP)], f0.at[pl.ds(0, DEEP), wide], down, s)

    loads[0].wait()
    loads[1].wait()

    spot = lax.broadcasted_iota(jnp.int32, (height, LANES), 1)
    low = [
        f0[pl.ds(DEEP, height), 0:LANES],
        pltpu.roll(flow[0, pl.ds(THIN, height), 0:LANES], 16, 1),
        pltpu.roll(flow[1, pl.ds(THIN, height), 0:LANES], 32, 1),
    ]
    tail = pl.ds(across - LANES, LANES)
    high = [
        f0[pl.ds(DEEP, height), tail],
        pltpu.roll(flow[0, pl.ds(THIN, height), tail], LANES - 16, 1),
        pltpu.roll(flow[1, pl.ds(THIN, height), tail], LANES - 32, 1),
    ]
    low_edge = jnp.where(spot < 16, low[0], jnp.where(spot < 32, low[1], low[2]))
    high_edge = jnp.where(spot >= 112, high[0], jnp.where(spot >= 96, high[1], high[2]))
    side[...] = jnp.where(spot < 64, low_edge, high_edge)

    for box, strip in ((from_right, left), (from_left, right))[: 2 if nx > 2 else 1]:
        send(side, box.at[pl.ds(DEEP, height)], g, strip)
        send(side.at[pl.ds(0, DEEP)], box.at[pl.ds(DEEP + height, DEEP)], up, strip)
        send(side.at[pl.ds(height - DEEP, DEEP)], box.at[pl.ds(0, DEEP)], down, strip)
    loads[2].wait()
    loads[3].wait()
    radius = parts[2]
    weight = escaped[...].astype(jnp.float32) * radius

    home_row = home_col // across
    home_at = home_col - home_row * across
    pick_lane = lax.broadcasted_iota(jnp.int32, (total, THIN + height), 1)
    pick = jnp.concatenate(
        [
            (pick_lane == home_row).astype(jnp.float32),
            (pick_lane == home_row + 1).astype(jnp.float32),
        ],
        axis=0,
    )
    slot_row = lax.broadcasted_iota(jnp.int32, (nb * CAP, total), 0)
    slot_hot = (slot_row == slot).astype(jnp.float32)
    band_row = lax.broadcasted_iota(jnp.int32, (nb, total), 0)
    own_hot = (band_row == own_band).astype(jnp.float32)
    past_hot = (band_row == past_band).astype(jnp.float32)
    land_row = land_col // across

    column = lax.broadcasted_iota(jnp.int32, (total, across), 1)
    this_column = column == home_at
    next_column = column == home_at + 1
    at_last = home_row == height - 1
    at_edge = home_at == across - 1
    fraction_y = parts[1] + 0.5
    fraction_x = parts[0] + 0.5

    def at(rows, mask):
        return jnp.sum(jnp.where(mask, rows, 0.0), axis=1, keepdims=True)

    inside = []
    for component in range(2):
        both = chosen(pick[:, :height], flow[component, pl.ds(THIN, height), wide])
        inside.append(
            [
                at(both[low : low + total], mask)
                for mask in (this_column, next_column)
                for low in (0, total)
            ]
        )

    def early(i, carry):
        row = pl.multiple_of(i * 8, 8)
        rows = pl.ds(row + DEEP - THIN, 8)
        f1[rows, wide] = row_term(f0, row + DEEP - THIN, wide, flow[1, pl.ds(row, 8), wide])
        return carry

    lax.fori_loop(2, height // 8, early, 0)

    for copy in halo[:2] + halo[4:]:
        copy.wait()

    spot = lax.broadcasted_iota(jnp.int32, (height + 2 * DEEP, LANES), 1)
    after = from_right[...]
    before = from_left[...] if nx > 2 else after
    end = pl.ds(across, LANES)
    f0[:, end] = jnp.where(spot < 64, after, before)
    inner = slice(DEEP - THIN, DEEP + height + THIN)
    spot, after, before = spot[inner], after[inner], before[inner]
    flow[0, :, end] = jnp.where(
        spot < 64, pltpu.roll(after, LANES - 16, 1), pltpu.roll(before, 16, 1)
    )
    flow[1, :, end] = jnp.where(
        spot < 64, pltpu.roll(after, LANES - 32, 1), pltpu.roll(before, 32, 1)
    )

    def mixture(component):
        low_low, high_low, low_high, high_high = inside[component]
        below = flow[component, pl.ds(THIN + height, THIN), wide][0:1]
        beyond = chosen(pick, flow[component, pl.ds(THIN, height + THIN), end])[:, 0:1]
        high_low = high_low + jnp.where(at_last, at(below, this_column), 0.0)
        high_high = high_high + jnp.where(at_last, at(below, next_column), 0.0)
        low_high = low_high + jnp.where(at_edge, beyond[:total], 0.0)
        high_high = high_high + jnp.where(at_edge, beyond[total:], 0.0)
        return (
            (1.0 - fraction_y) * (1.0 - fraction_x) * low_low
            + fraction_y * (1.0 - fraction_x) * high_low
            + (1.0 - fraction_y) * fraction_x * low_high
            + fraction_y * fraction_x * high_high
        )

    new_x = parts[0] + STEP * mixture(0)
    new_y = parts[1] + STEP * mixture(1)

    payload = chosen(slot_hot, jnp.concatenate([new_x, new_y, radius, weight], axis=1))
    for k in range(FIELDS):
        packed[pl.ds(k, nb * CAP, stride=FIELDS), :] = payload[:, k * LANES : (k + 1) * LANES]

    per = CAP * FIELDS
    mine = pl.ds(pl.multiple_of(g * per, per), per)

    def pay_copy(k):
        peer = lax.rem(g + k, nb)
        return pltpu.make_async_remote_copy(
            src_ref=packed.at[pl.ds(pl.multiple_of(peer * per, per), per)],
            dst_ref=moved_hbm.at[mine],
            send_sem=pay_send.at[k],
            recv_sem=pay_recv.at[k],
            device_id=(peer, s),
            device_id_type=MESH,
        )

    def rec_copy(k):
        peer = lax.rem(g + k, nb)
        return pltpu.make_async_remote_copy(
            src_ref=records.at[peer],
            dst_ref=rec_same.at[g],
            send_sem=rec_send.at[k],
            recv_sem=rec_recv.at[k],
            device_id=(peer, s),
            device_id_type=MESH,
        )

    def left_copy(k):
        peer = lax.rem(g + k, nb)
        return pltpu.make_async_remote_copy(
            src_ref=records.at[peer],
            dst_ref=rec_left.at[g],
            send_sem=left_send.at[k],
            recv_sem=left_recv.at[k],
            device_id=(peer, right),
            device_id_type=MESH,
        )

    def start_far(k, carry):
        pay_copy(k).start()
        return carry

    def start_records(k, carry):
        rec_copy(k).start()
        left_copy(k).start()
        return carry

    lax.fori_loop(1, nb, start_far, 0)

    gy = new_y + 0.5
    gx = new_x + 0.5

    def over(rows):
        return jnp.sum(rows, axis=1, keepdims=True)

    columns = (
        land_row.astype(jnp.float32),
        (land_col - land_row * across).astype(jnp.float32),
        over(weight * (1.0 - gy) * (1.0 - gx)),
        over(weight * gy * (1.0 - gx)),
        over(weight * (1.0 - gy) * gx),
        over(weight * gy * gx),
    )
    spot = lax.broadcasted_iota(jnp.int32, (total, LANES), 1)
    table = jnp.zeros((total, LANES), jnp.float32)
    for k, one in enumerate(columns):
        table = jnp.where(spot // (2 * CAP) == k, one, table)
    place = spot % (2 * CAP)
    sheet = chosen(own_hot, jnp.where(place == rank_col, table, 0.0)) + chosen(
        past_hot, jnp.where(place == rank_col + CAP, table, 0.0)
    )
    for band in range(nb):
        records[band] = sheet[band : band + 1]

    left_copy(0).start()
    lax.fori_loop(1, nb, start_records, 0)
    own = [
        pltpu.make_async_copy(packed.at[mine], moved_hbm.at[mine], own_sem.at[0]),
        pltpu.make_async_copy(records.at[g], rec_same.at[g], own_sem.at[1]),
    ]
    for copy in own:
        copy.start()

    for copy in halo[2:4]:
        copy.wait()

    def first(i, carry):
        row = pl.multiple_of(i * 8, 8)
        here, term = step_term(
            f0, row + DEEP - THIN, flow[0, pl.ds(row, 8), :], flow[1, pl.ds(row, 8), :]
        )
        f1[pl.ds(row + DEEP - THIN, 8), :] = here + STEP * term
        return carry

    def first_inner(i, carry):
        row = pl.multiple_of(i * 8, 8)
        rows = pl.ds(row + DEEP - THIN, 8)
        here = f0[rows, :]
        along_x = column_term(here, flow[0, pl.ds(row, 8), :])
        end_y = row_term(f0, row + DEEP - THIN, end, flow[1, pl.ds(row, 8), end])
        along_y = jnp.concatenate([f1[rows, wide], end_y], axis=1)
        f1[rows, :] = here - STEP * (along_x + along_y)
        return carry

    chunks = (height + 2 * THIN) // 8
    lax.fori_loop(0, 2, first, 0)
    lax.fori_loop(2, chunks - 2, first_inner, 0)
    lax.fori_loop(chunks - 2, chunks, first, 0)

    def second(i, carry):
        row = pl.multiple_of(i * 8, 8)
        here, term = step_term(
            f1, row + DEEP - THIN, flow[0, pl.ds(row, 8), :], flow[1, pl.ds(row, 8), :]
        )
        at = pl.ds(row + DEEP - THIN, 8)
        f2[at, :] = 0.75 * f0[at, :] + 0.25 * (here + STEP * term)
        return carry

    lax.fori_loop(0, (height + 2 * THIN) // 8, second, 0)

    def third(i, carry):
        row = pl.multiple_of(i * 8, 8)
        at = pl.ds(row + THIN, 8)
        here, term = step_term(f2, row + DEEP, flow[0, at, :], flow[1, at, :])
        value = f0[pl.ds(row + DEEP, 8), :] / 3.0 + 2.0 / 3.0 * (here + STEP * term)
        out_ref[pl.ds(row, 8), :] = value[:, :across]
        return carry

    lax.fori_loop(0, height // 8, third, 0)

    for copy in own:
        copy.wait()
    left_copy(0).wait()

    def finish_far(k, carry):
        rec_copy(k).wait()
        left_copy(k).wait()
        return carry

    lax.fori_loop(1, nb, finish_far, 0)

    row_lane = lax.broadcasted_iota(jnp.int32, (nb, LANES), 1).astype(jnp.float32)
    lane_out = lax.broadcasted_iota(jnp.int32, (nb, across), 1).astype(jnp.float32)
    spread = 2 * CAP

    def slots_of(box):
        for j in range(spread):
            fields = [box[:, k * spread + j : k * spread + j + 1] for k in range(6)]
            if j >= CAP:
                fields[0] = fields[0] - float(height)
            yield fields

    def laid(hots, rows):
        hot = jnp.transpose(jnp.concatenate(hots, axis=0))[:height]
        return chosen(hot, jnp.concatenate(rows, axis=0))

    hots, rows = [], []
    for row, col, low_low, high_low, low_high, high_high in slots_of(
        jnp.concatenate([rec_same[k] for k in range(nb)], axis=0)
    ):
        here, beside = lane_out == col, lane_out == col + 1.0
        hots += [(row_lane == row).astype(jnp.float32), (row_lane == row + 1.0).astype(jnp.float32)]
        rows += [
            jnp.where(here, low_low, jnp.where(beside, low_high, 0.0)),
            jnp.where(here, high_low, jnp.where(beside, high_high, 0.0)),
        ]
    out_ref[...] += laid(hots, rows)
    hots, rows = [], []
    for row, col, low_low, high_low, low_high, high_high in slots_of(
        jnp.concatenate([rec_left[k] for k in range(nb)], axis=0)
    ):
        spill = (col == float(across - 1)) & (row_lane == 0.0)
        hots += [(row_lane == row).astype(jnp.float32), (row_lane == row + 1.0).astype(jnp.float32)]
        rows += [jnp.where(spill, low_high, 0.0), jnp.where(spill, high_high, 0.0)]
    out_ref[:, 0:LANES] += laid(hots, rows)

    def finish_pay(k, carry):
        pay_copy(k).wait()
        return carry

    lax.fori_loop(1, nb, finish_pay, 0)


def settle(level_ref, moved_ref, level_hbm, moved_hbm, sem):
    copies = [
        pltpu.make_async_copy(level_ref, level_hbm, sem.at[0]),
        pltpu.make_async_copy(moved_ref, moved_hbm, sem.at[1]),
    ]
    for copy in copies:
        copy.start()
    for copy in copies:
        copy.wait()


def shards(nb, nx, level_set, velocity, particles, escaped, home, land, dest, count):
    height, across = level_set.shape
    total, kinds, per_block = particles.shape
    width = across + LANES
    rows = nb * CAP * FIELDS
    halos = 10 if nx > 2 else 7
    vmem = pl.BlockSpec(memory_space=pltpu.VMEM)
    f32 = jnp.float32
    dma = pltpu.SemaphoreType.DMA
    level, moved = pl.pallas_call(
        functools.partial(kernel, nb, nx),
        out_shape=(
            pltpu.VMEM((height, across), f32),
            pltpu.VMEM((rows, per_block), f32),
        ),
        in_specs=[pl.BlockSpec(memory_space=pltpu.HBM)] * 8,
        out_specs=(vmem, vmem),
        scratch_shapes=[
            pltpu.VMEM((height + 2 * DEEP, width), f32),
            pltpu.VMEM((2, height + 2 * THIN, width), f32),
            pltpu.VMEM((height + 2 * DEEP, width), f32),
            pltpu.VMEM((height + 2 * DEEP, width), f32),
            pltpu.VMEM((height, LANES), f32),
            pltpu.VMEM((height + 2 * DEEP, LANES), f32),
            pltpu.VMEM((height + 2 * DEEP, LANES), f32),
            pltpu.VMEM((kinds, total, per_block), f32),
            pltpu.VMEM(escaped.shape, jnp.int32),
            pltpu.VMEM(home.shape, jnp.int32),
            pltpu.VMEM(land.shape, jnp.int32),
            pltpu.VMEM(dest.shape, jnp.int32),
            pltpu.SMEM(count.shape, jnp.int32),
            pltpu.VMEM((rows, per_block), f32),
            pltpu.VMEM((nb, 1, LANES), f32),
            pltpu.VMEM((nb, 1, LANES), f32),
            pltpu.VMEM((nb, 1, LANES), f32),
            dma((8,)),
            dma((halos,)),
            dma((halos,)),
            dma((nb,)),
            dma((nb,)),
            dma((nb,)),
            dma((nb,)),
            dma((nb,)),
            dma((nb,)),
            dma((2,)),
        ],
        compiler_params=pltpu.CompilerParams(collective_id=0, has_side_effects=True),
    )(
        level_set,
        velocity,
        jnp.transpose(particles, (1, 0, 2)),
        escaped,
        home,
        land,
        dest,
        count,
    )
    level, moved = pl.pallas_call(
        settle,
        out_shape=(
            jax.ShapeDtypeStruct((height, across), f32),
            jax.ShapeDtypeStruct((rows, per_block), f32),
        ),
        in_specs=[vmem, vmem],
        out_specs=(pl.BlockSpec(memory_space=pl.ANY),) * 2,
        scratch_shapes=[dma((2,))],
    )(
        pltpu.with_memory_space_constraint(level, pltpu.VMEM),
        pltpu.with_memory_space_constraint(moved, pltpu.VMEM),
    )
    return level, moved.reshape(nb * CAP, FIELDS, per_block)


def solution(mesh):
    in_specs = (
        P("gy", "gx"),
        P(None, "gy", "gx"),
        P(("gy", "gx"), None, None),
        P(("gy", "gx"), None),
        P(("gy", "gx")),
        P(("gy", "gx")),
        P(("gy", "gx")),
        P(("gy", "gx")),
    )
    out_specs = (P("gy", "gx"), P(("gy", "gx"), None, None))
    body = functools.partial(shards, mesh.shape["gy"], mesh.shape["gx"])
    return jax.shard_map(body, mesh=mesh, in_specs=in_specs, out_specs=out_specs, check_vma=False)
```
